512 devices in a mesh: vrow: 2 (over y_lo), vcol: 8 (over z), pix: 32 (over x, y_hi, core).
Axes of the slice: x: 4, y: 8 (y_hi: 4, y_lo: 2; y = y_hi * 2 + y_lo), z: 8, core: 2. Of those that a mesh axis runs over, the one named last changes fastest.
Arguments:
- features: bfloat16 [16, 16, 64, 4096], P('vrow', 'vcol', None, 'pix'), may hold values from -400 to 400
- out_cotangent: bfloat16 [16, 16, 64, 4096], P('vrow', 'vcol', None, 'pix'), may hold values from -6 to 6
- norm_gain: float32 [64], replicated, may hold values from 0.25 to 1.75
- query_proj: bfloat16 [64, 64], replicated, may hold values from -0.75 to 0.75
- keyval_proj: bfloat16 [64, 128], replicated, may hold values from -0.75 to 0.75
- output_proj: bfloat16 [64, 64], replicated, may hold values from -0.75 to 0.75
Outputs:
- features_grad: bfloat16 [16, 16, 64, 4096], P('vrow', 'vcol', None, 'pix')
- query_proj_grad: float32 [64, 64], replicated
- keyval_proj_grad: float32 [64, 128], replicated
- output_proj_grad: float32 [64, 64], replicated
- norm_gain_grad: float32 [64], replicated
The draws below stay inside these ranges and needn't reach their ends.
All inputs are finite; a program needn't handle non-finite values.
Results may differ from the reference program's by a relative error of at most 0.0085.
Values may be sent and summed in bfloat16 or wider, within the bound.
No kernel may reach another device: no remote copies, remote signals or barrier semaphores. Data moves between devices by JAX's collectives and lax.ppermute only.
A program may use at most 64 MiB of HBM per device.

```python
import math
import jax
import jax.numpy as jnp
from jax import lax

D = 64
HEADS = 4
VIEW_ROWS = 16
VIEW_COLS = 16
PIX_DEV = 128
PIXELS = 4096
TOKENS = 1048576


def draw_features(key, part):
    noise_key, token_key, channel_key = jax.random.split(key, 3)
    full_shape = (VIEW_ROWS, VIEW_COLS, D, PIXELS)
    base_noise = jnp.clip(jax.random.normal(noise_key, full_shape, jnp.float32), -4.0, 4.0)
    token_scale = jnp.exp(jax.random.uniform(token_key, (VIEW_ROWS, VIEW_COLS, 1, PIXELS), jnp.float32) * math.log(10.0))
    channel_scale = jnp.exp(jax.random.uniform(channel_key, (1, 1, D, 1), jnp.float32) * math.log(10.0))
    return (base_noise * token_scale * channel_scale).astype(jnp.bfloat16)


def levels(stream_key, dims, shards, low, largest):
    level, own = 1.0, jax.random.fold_in(stream_key, 6)
    for axis_at, blocks in shards:
        steps = jnp.exp(jax.random.uniform(jax.random.fold_in(own, axis_at), (blocks,), jnp.float32, low / len(shards), largest / len(shards)))
        level = level * jnp.repeat(steps, dims[axis_at] // blocks).reshape([-1 if axis == axis_at else 1 for axis in range(len(dims))])
    return level


def centred(stream_key, extent, width, most, cuts=(), kind=jnp.bfloat16):
    entries = width * jax.random.normal(stream_key, extent, jnp.float32)
    if cuts:
        entries = entries * levels(stream_key, extent, cuts, -0.22, 0.18)
    return jnp.clip(entries, -most, most).astype(kind)


def setup_inputs(seed: int = 0) -> dict:
    key_list = jax.random.split(jax.random.key(seed), 7)
    features = draw_features(jax.random.fold_in(key_list[6], 71), 0)
    out_cotangent = centred(key_list[1], (VIEW_ROWS, VIEW_COLS, D, PIXELS), 1.0, 6.0, ((0, 2), (1, 8), (3, 32)))
    norm_gain = jnp.clip(1.0 + 0.15 * jax.random.normal(key_list[2], (D,), jnp.float32), 0.25, 1.75)
    query_proj = centred(key_list[3], (D, D), D ** -0.5, 0.75)
    keyval_proj = centred(key_list[4], (D, 2 * D), D ** -0.5, 0.75)
    output_proj = centred(key_list[5], (D, D), D ** -0.5, 0.75)
    return dict(features=features, out_cotangent=out_cotangent, norm_gain=norm_gain, query_proj=query_proj, keyval_proj=keyval_proj, output_proj=output_proj)


EPSILON = 1e-06
precise = lax.Precision.HIGHEST

def normalize(features, norm_gain):
    values = features.astype(jnp.float32)
    inv_norm = lax.rsqrt(lax.optimization_barrier(jnp.mean(values * values, axis=2, keepdims=True)) + EPSILON)
    scaled = values * inv_norm
    normed = (scaled * norm_gain[None, None, :, None]).astype(jnp.bfloat16)
    return (normed, scaled, inv_norm)

def unit_rows(raw_proj):
    inv_norm = lax.rsqrt(lax.optimization_barrier(jnp.mean(raw_proj * raw_proj, axis=2, keepdims=True)) + EPSILON)
    return (raw_proj * inv_norm, inv_norm)

def unit_back(unit_vals, inv_norm, upstream):
    return inv_norm * (upstream - unit_vals * lax.optimization_barrier(jnp.mean(upstream * unit_vals, axis=2, keepdims=True)))

def project(normed, weight):
    return jnp.einsum('uvdp,de->uvep', normed.astype(jnp.float32), weight.astype(jnp.float32), precision=precise)

def attention(query, keyval_pad):
    view_rows, view_cols, channels, pixels = query.shape
    head_size = channels // HEADS
    query_heads = query.reshape(view_rows, view_cols, HEADS, head_size, pixels)
    exp_total = jnp.zeros((view_rows, view_cols, HEADS, pixels), jnp.float32)
    weighted = jnp.zeros(query_heads.shape, jnp.float32)
    for row_shift in range(5):
        for col_shift in range(5):
            window = keyval_pad[row_shift:row_shift + view_rows, col_shift:col_shift + view_cols]
            key_heads = window[:, :, :channels].reshape(query_heads.shape)
            values = window[:, :, channels:].reshape(query_heads.shape)
            weight = jnp.exp(lax.optimization_barrier(jnp.sum(query_heads * key_heads, axis=3)) * head_size ** (-0.5))
            exp_total = exp_total + weight
            weighted = weighted + weight[:, :, :, None] * values
    return (weighted / exp_total[:, :, :, None]).reshape(view_rows, view_cols, channels, pixels)

def block_pass(features, cotangent, norm_gain, query_proj, keyval_proj, output_proj):
    normed, scaled, inv_norm = normalize(features, norm_gain)
    channels = features.shape[2]
    raw_query = project(normed, query_proj)
    unit_query, query_inv = unit_rows(raw_query)
    query = lax.optimization_barrier(unit_query.astype(jnp.bfloat16)).astype(jnp.float32)
    raw_keyval = project(normed, keyval_proj)
    unit_key, key_inv = unit_rows(raw_keyval[:, :, :channels])
    keyval = jnp.concatenate([unit_key, raw_keyval[:, :, channels:]], axis=2)
    keyval = lax.optimization_barrier(keyval.astype(jnp.bfloat16)).astype(jnp.float32)
    keyval_pad = jnp.pad(keyval, ((2, 2), (2, 2), (0, 0), (0, 0)))
    attended, pullback = jax.vjp(attention, query, keyval_pad)
    mixed_out = attended.astype(jnp.bfloat16)
    cot_float = cotangent.astype(jnp.float32)
    out_grad = jnp.einsum('uvep,de->uvdp', cot_float, output_proj.astype(jnp.float32), precision=precise)
    query_grad, keyval_pad_grad = pullback(out_grad)
    keyval_grad = keyval_pad_grad[2:-2, 2:-2]
    raw_query_grad = unit_back(unit_query, query_inv, query_grad)
    raw_keyval_grad = jnp.concatenate([unit_back(unit_key, key_inv, keyval_grad[:, :, :channels]), keyval_grad[:, :, channels:]], axis=2)
    normed_grad = jnp.einsum('uvep,de->uvdp', raw_query_grad, query_proj.astype(jnp.float32), precision=precise)
    normed_grad = normed_grad + jnp.einsum('uvep,de->uvdp', raw_keyval_grad, keyval_proj.astype(jnp.float32), precision=precise)
    normed_float = normed.astype(jnp.float32)
    query_part = jnp.einsum('uvdp,uvep->de', normed_float, raw_query_grad, precision=precise)
    keyval_part = jnp.einsum('uvdp,uvep->de', normed_float, raw_keyval_grad, precision=precise)
    output_part = jnp.einsum('uvdp,uvep->de', mixed_out.astype(jnp.float32), cot_float, precision=precise)
    scaled_grad = normed_grad * norm_gain[None, None, :, None]
    gain_part = lax.optimization_barrier(jnp.sum(normed_grad * scaled, axis=(0, 1, 3)))
    branch = inv_norm * (scaled_grad - scaled * lax.optimization_barrier(jnp.mean(scaled_grad * scaled, axis=2, keepdims=True)))
    features_grad = (cot_float + branch).astype(jnp.bfloat16)
    return (features_grad, (query_part, keyval_part, output_part, gain_part))

def reference(features, out_cotangent, norm_gain, query_proj, keyval_proj, output_proj):
    block_size = min(PIX_DEV, 128)
    block_count = PIXELS // block_size

    def scan_step(weight_sums, block_index):
        first_pixel = (block_index * block_size).astype(jnp.int32)
        feature_block = lax.dynamic_slice_in_dim(features, first_pixel, block_size, 3)
        cotangent_block = lax.dynamic_slice_in_dim(out_cotangent, first_pixel, block_size, 3)
        grad_block, parts = block_pass(feature_block, cotangent_block, norm_gain, query_proj, keyval_proj, output_proj)
        return (tuple((summed + addend for summed, addend in zip(weight_sums, parts))), grad_block)
    initial = (jnp.zeros((D, D), jnp.float32), jnp.zeros((D, 2 * D), jnp.float32), jnp.zeros((D, D), jnp.float32), jnp.zeros((D,), jnp.float32))
    weight_sums, grad_blocks = lax.scan(scan_step, initial, jnp.arange(block_count, dtype=jnp.int32))
    features_grad = jnp.moveaxis(grad_blocks, 0, 3).reshape(VIEW_ROWS, VIEW_COLS, D, PIXELS)
    factor = 1.0 / math.sqrt(TOKENS)
    return (features_grad, weight_sums[0] * factor, weight_sums[1] * factor, weight_sums[2] * factor, weight_sums[3] * factor)
```

```python
import math

import jax
import jax.numpy as jnp
from jax import lax
from jax.experimental import pallas as pl
from jax.experimental.pallas import tpu as pltpu
from jax.sharding import PartitionSpec as P

HEADS = 4
SIZE = 16
CH = 64
ROWS = 8
COLS = 2
PIX = 128
S = 13
EPSILON = 1e-06
SCALE = SIZE ** (-0.5)
F32 = jnp.float32
BF16 = jnp.bfloat16

VM = pl.BlockSpec(memory_space=pltpu.VMEM)
SM = pl.BlockSpec(memory_space=pltpu.SMEM)


def inv_rms(values):
    return lax.rsqrt(jnp.mean(values * values, axis=0, keepdims=True) + EPSILON)


def total(terms):
    terms = list(terms)
    while len(terms) > 1:
        terms = [a + b for a, b in zip(terms[::2], terms[1::2])] + (
            [terms[-1]] if len(terms) % 2 else []
        )
    return terms[0]


def normed_pair(ref, row, gain):
    out = []
    for j in range(2):
        values = ref[row, j].astype(F32)
        out.append((values * inv_rms(values) * gain).astype(BF16))
    return jnp.concatenate(out, axis=1)


def put(ref, col, row, values):
    ref[col, pl.ds(row, values.shape[0], stride=S), :] = values


def take(ref, col, start):
    return ref[col, pl.ds(start, ROWS), :]


def each_piece(own, left, right, row_halo, left_corner, right_corner, halo_row, visit):
    def big(row, carry):
        visit(own, row, row + 2, 2)
        visit(left, row, row + 2, 0)
        visit(right, row, row + 2, 4)
        return carry

    def small(row, carry):
        visit(row_halo, row, row + halo_row, 2)
        visit(left_corner, row, row + halo_row, 0)
        visit(right_corner, row, row + halo_row, 4)
        return carry

    lax.fori_loop(0, ROWS, big, 0)
    lax.fori_loop(0, 2, small, 0)


def halo_start(side_ref):
    side = side_ref[0]
    return 10 - 10 * side, 10 * side


def clear_rows(refs, row):
    for ref in refs:
        zeros = jnp.zeros((ref.shape[1] // S, PIX), F32)
        for col in range(6):
            put(ref, col, row, zeros)
            put(ref, col, row + 1, zeros)


def forward_kernel(
    side, own, left, right, row_halo, left_corner, right_corner, cot, gain, w_in, w_out,
    qs, ks, vs, q_inv, k_inv, weights, prob_grads, attended, stats, ogs,
):
    halo_row, clear_row = halo_start(side)
    clear_rows((qs, ks, vs), clear_row)
    gain_full = gain[...]
    w_full = w_in[...]

    def visit(ref, row, to_row, col):
        normed = normed_pair(ref, row, gain_full)
        raw = jnp.dot(w_full, normed, preferred_element_type=F32)
        for j in range(2):
            part = raw[:, j * PIX : (j + 1) * PIX]
            query, key, value = part[:CH], part[CH : 2 * CH], part[2 * CH :]
            query_scale, key_scale = inv_rms(query), inv_rms(key)
            put(qs, col + j, to_row, (query * query_scale).astype(BF16).astype(F32))
            put(ks, col + j, to_row, (key * key_scale).astype(BF16).astype(F32))
            put(vs, col + j, to_row, value.astype(BF16).astype(F32))
            if ref is own:
                q_inv[j, pl.ds(row, 1), :] = query_scale
                k_inv[j, pl.ds(row, 1), :] = key_scale

    each_piece(own, left, right, row_halo, left_corner, right_corner, halo_row, visit)

    w_o = w_out[...]

    def own_out(row, carry):
        both = jnp.concatenate([cot[row, 0], cot[row, 1]], axis=1)
        og = jnp.dot(w_o, both, preferred_element_type=F32)
        for j in range(2):
            put(ogs, j, row, og[:, j * PIX : (j + 1) * PIX])
        return carry

    lax.fori_loop(0, ROWS, own_out, 0)

    def attend(step, carry):
        col, head = step // HEADS, step % HEADS
        base = head * (SIZE * S)
        query = [take(qs, col + 2, base + d * S + 2) * SCALE for d in range(SIZE)]
        og = [take(ogs, col, base + d * S) for d in range(SIZE)]
        acc = [jnp.zeros((ROWS, PIX), F32)] * SIZE
        exp_total = jnp.zeros((ROWS, PIX), F32)
        spread = jnp.zeros((ROWS, PIX), F32)
        for j in range(5):
            for i in range(5):
                key = [take(ks, col + j, base + d * S + i) for d in range(SIZE)]
                weight = jnp.exp(total(a * b for a, b in zip(query, key)))
                value = [take(vs, col + j, base + d * S + i) for d in range(SIZE)]
                prob_grad = total(a * b for a, b in zip(og, value))
                acc = [a + weight * b for a, b in zip(acc, value)]
                exp_total = exp_total + weight
                spread = spread + weight * prob_grad
                weights[step, 5 * j + i] = weight
                prob_grads[step, 5 * j + i] = prob_grad
        inv_total = 1.0 / exp_total
        for d in range(SIZE):
            attended[col, pl.ds(pl.multiple_of((head * SIZE + d) * ROWS, ROWS), ROWS), :] = (
                acc[d] * inv_total
            )
        stats[pl.ds(col * 8 + head, ROWS, stride=16), :] = inv_total
        stats[pl.ds(col * 8 + 4 + head, ROWS, stride=16), :] = spread * inv_total
        return carry

    lax.fori_loop(0, COLS * HEADS, attend, 0)


def unit_back(unit, scale, upstream):
    mean = jnp.sum(upstream * unit, axis=0, keepdims=True) * (1.0 / CH)
    return scale[None] * (upstream - unit * mean)


def own_channels(ref, col):
    return jnp.stack([take(ref, col + 2, d * S + 2) for d in range(CH)], axis=0)


def query_kernel(qs, ks, weights, prob_grads, stats, attended, cot, q_inv, raw_query, out_part, grads):
    def query_one(step, carry):
        col, head = step // HEADS, step % HEADS
        base = head * (SIZE * S)
        inv_total = stats[pl.ds(col * 8 + head, ROWS, stride=16), :]
        spread = stats[pl.ds(col * 8 + 4 + head, ROWS, stride=16), :]
        inv_total = inv_total * SCALE
        acc = [jnp.zeros((ROWS, PIX), F32)] * SIZE
        for j in range(5):
            for i in range(5):
                o = 5 * j + i
                score_grad = weights[step, o] * inv_total * (prob_grads[step, o] - spread)
                acc = [a + score_grad * take(ks, col + j, base + d * S + i) for d, a in enumerate(acc)]
        for d in range(SIZE):
            grads[col, head * SIZE + d] = acc[d]
        return carry

    lax.fori_loop(0, COLS * HEADS, query_one, 0)

    def finish(col, carry):
        raw = unit_back(own_channels(qs, col), q_inv[col], grads[col])
        raw_query[col] = raw.reshape(CH * ROWS, PIX)
        return carry

    lax.fori_loop(0, COLS, finish, 0)

    def out_grads(row, acc):
        mixed = [attended[j, pl.ds(row, CH, stride=ROWS), :].astype(BF16) for j in range(2)]
        return acc + lax.dot_general(
            jnp.concatenate(mixed, axis=1),
            jnp.concatenate([cot[row, 0], cot[row, 1]], axis=1),
            (((1,), (1,)), ((), ())),
            preferred_element_type=F32,
        )

    out_part[...] = lax.fori_loop(0, ROWS, out_grads, jnp.zeros((CH, CH), F32))


def key_kernel(
    side, qs, ks, vs, k_inv, raw_query, out_part,
    own, left, right, row_halo, left_corner, right_corner,
    own_st, left_st, right_st, row_st, left_corner_st, right_corner_st,
    feats, gain, w_back, w_out,
    feats_grad, weight_sums,
    ogs, sts, grads, raws,
):
    halo_row, clear_row = halo_start(side)
    clear_rows((ogs, sts), clear_row)
    w_o = w_out[...]

    def visit(ref, row, to_row, col):
        both = jnp.concatenate([ref[row, 0], ref[row, 1]], axis=1)
        og = jnp.dot(w_o, both, preferred_element_type=F32)
        for j in range(2):
            put(ogs, col + j, to_row, og[:, j * PIX : (j + 1) * PIX])

    each_piece(own, left, right, row_halo, left_corner, right_corner, halo_row, visit)

    def visit_stats(ref, row, to_row, col):
        for j in range(2):
            put(sts, col + j, to_row, ref[row, j])

    each_piece(
        own_st, left_st, right_st, row_st, left_corner_st, right_corner_st, halo_row, visit_stats
    )

    def key_one(step, carry):
        col, head = step // HEADS, step % HEADS
        base = head * (SIZE * S)
        key_acc = [jnp.zeros((ROWS, PIX), F32)] * SIZE
        value_acc = [jnp.zeros((ROWS, PIX), F32)] * SIZE
        for j in range(5):
            for i in range(5):
                query = [take(qs, col + j, base + d * S + i) for d in range(SIZE)]
                key = [take(ks, col + 2, base + d * S + 2) for d in range(SIZE)]
                inv_total = take(sts, col + j, head * S + i)
                spread = take(sts, col + j, (head + HEADS) * S + i)
                score = total(a * b for a, b in zip(query, key))
                prob = jnp.exp(score * SCALE) * inv_total
                og = [take(ogs, col + j, base + d * S + i) for d in range(SIZE)]
                value = [take(vs, col + 2, base + d * S + 2) for d in range(SIZE)]
                prob_grad = total(a * b for a, b in zip(og, value))
                score_grad = prob * (prob_grad - spread)
                key_acc = [a + score_grad * b for a, b in zip(key_acc, query)]
                value_acc = [a + prob * b for a, b in zip(value_acc, og)]
        for d in range(SIZE):
            grads[col, head * SIZE + d] = key_acc[d] * SCALE
            raws[col, pl.ds(pl.multiple_of((2 * CH + head * SIZE + d) * ROWS, ROWS), ROWS), :] = (
                value_acc[d]
            )
        return carry

    lax.fori_loop(0, COLS * HEADS, key_one, 0)

    def finish(col, carry):
        raw = unit_back(own_channels(ks, col), k_inv[col], grads[col])
        raws[col, CH * ROWS : 2 * CH * ROWS, :] = raw.reshape(CH * ROWS, PIX)
        raws[col, 0 : CH * ROWS, :] = raw_query[col]
        return carry

    lax.fori_loop(0, COLS, finish, 0)

    gain_full = gain[...]
    w_b = w_back[...]

    def view_row(row, acc):
        raw = jnp.concatenate(
            [raws[j, pl.ds(row, 3 * CH, stride=ROWS), :].astype(BF16) for j in range(2)], axis=1
        )
        normed_grad = jnp.dot(w_b, raw, preferred_element_type=F32)
        normed = []
        for j in range(2):
            values = feats[row, j].astype(F32)
            inv_norm = inv_rms(values)
            scaled = values * inv_norm
            normed.append((scaled * gain_full).astype(BF16))
            scaled_grad = normed_grad[:, j * PIX : (j + 1) * PIX] * gain_full
            mean = jnp.mean(scaled_grad * scaled, axis=0, keepdims=True)
            branch = inv_norm * (scaled_grad - scaled * mean)
            feats_grad[row, j] = (own[row, j].astype(F32) + branch).astype(BF16)
        return acc + lax.dot_general(
            jnp.concatenate(normed, axis=1),
            raw,
            (((1,), (1,)), ((), ())),
            preferred_element_type=F32,
        )

    sums = lax.fori_loop(0, ROWS, view_row, jnp.zeros((CH, 3 * CH), F32))
    weight_sums[0:CH, :] = sums[:, CH:]
    weight_sums[CH : 2 * CH, :] = jnp.concatenate([sums[:, :CH], out_part[...]], axis=1)


def call(kernel, outs, scratch, flops, *operands):
    return pl.pallas_call(
        kernel,
        out_shape=[jax.ShapeDtypeStruct(shape, dtype) for shape, dtype in outs],
        in_specs=[SM if x.dtype == jnp.int32 else VM for x in operands],
        out_specs=[VM] * len(outs),
        scratch_shapes=[pltpu.VMEM(shape, F32) for shape in scratch],
        compiler_params=pltpu.CompilerParams(vmem_limit_bytes=40 * 1024 * 1024),
        cost_estimate=pl.CostEstimate(flops=flops, bytes_accessed=1000000, transcendentals=0),
    )(*operands)


def neighbours(shard, row_edge):
    rows, cols = lax.axis_size("vrow"), lax.axis_size("vcol")
    up = [(i, i + 1) for i in range(cols - 1)]
    down = [(j, i) for i, j in up]
    cross = [(0, 1), (1, 0)]
    diag_up = [(a * cols + i, b * cols + j) for a, b in cross for i, j in up]
    diag_down = [(a * cols + i, b * cols + j) for a, b in cross for i, j in down]
    left = lax.ppermute(shard, "vcol", up)
    right = lax.ppermute(shard, "vcol", down)
    left_corner = lax.ppermute(row_edge, ("vrow", "vcol"), diag_up)
    right_corner = lax.ppermute(row_edge, ("vrow", "vcol"), diag_down)
    row_halo = lax.ppermute(row_edge, "vrow", cross)
    return left, right, row_halo, left_corner, right_corner


def sum_everywhere(values):
    group = ("vrow", "vcol")
    count, pix_count = lax.axis_size("vrow") * lax.axis_size("vcol"), lax.axis_size("pix")
    shares = lax.all_to_all(values.reshape(count, -1, PIX), group, 0, 0)
    share = jnp.sum(shares, axis=0)
    copies = jnp.broadcast_to(share[None], (pix_count,) + share.shape)
    share = jnp.sum(lax.all_to_all(copies, "pix", 0, 0), axis=0)
    copies = jnp.broadcast_to(share[None], (count,) + share.shape)
    return lax.all_to_all(copies, group, 0, 0).reshape(values.shape)


def body(features, out_cotangent, norm_gain, query_proj, keyval_proj, output_proj):
    vrow = lax.axis_index("vrow").astype(jnp.int32)
    side = vrow.reshape(1)
    edge_start = 6 - 6 * vrow

    def edge(values):
        return lax.dynamic_slice_in_dim(values, edge_start, 2, 0)

    feat_halo = neighbours(features, edge(features))
    cot_halo = neighbours(out_cotangent, edge(out_cotangent))

    gain = jnp.broadcast_to(norm_gain[:, None], (CH, PIX))
    w_back = jnp.concatenate([query_proj, keyval_proj], axis=1)
    w_in = w_back.T

    padded = ((6, CH * S, PIX), F32)
    lanes = ((COLS, ROWS, PIX), F32)
    offsets = ((COLS * HEADS, 25, ROWS, PIX), F32)
    channels = ((COLS, CH * ROWS, PIX), F32)
    qs, ks, vs, q_inv, k_inv, weights, prob_grads, attended, stats = call(
        forward_kernel,
        [padded, padded, padded, lanes, lanes, offsets, offsets, channels, ((ROWS * 16, PIX), F32)],
        [(COLS, CH * S, PIX)],
        4000000,
        side, features, *feat_halo, out_cotangent, gain, w_in, output_proj,
    )
    stats_view = stats.reshape(ROWS, COLS, 8, PIX)
    stats_halo = neighbours(stats_view, edge(stats_view))
    raw_query, out_part = call(
        query_kernel,
        [channels, ((CH, CH), F32)],
        [(COLS, CH, ROWS, PIX)],
        4000000,
        qs, ks, weights, prob_grads, stats, attended, out_cotangent, q_inv,
    )
    features_grad, weight_sums = call(
        key_kernel,
        [(features.shape, BF16), ((2 * CH, PIX), F32)],
        [(6, CH * S, PIX), (6, 8 * S, PIX), (COLS, CH, ROWS, PIX), (COLS, 3 * CH * ROWS, PIX)],
        4000000,
        side, qs, ks, vs, k_inv, raw_query, out_part,
        out_cotangent, *cot_halo, stats_view, *stats_halo,
        features, gain, w_back, output_proj,
    )
    tokens_all = (
        ROWS * COLS * PIX
        * lax.axis_size("vrow") * lax.axis_size("vcol") * lax.axis_size("pix")
    )
    sums = sum_everywhere(weight_sums) * (1.0 / math.sqrt(tokens_all))
    keyval_grad, query_grad, output_grad = sums[:CH], sums[CH:, :CH], sums[CH:, CH:]
    gain_grad = (
        jnp.sum(query_grad * query_proj.astype(F32), axis=1)
        + jnp.sum(keyval_grad * keyval_proj.astype(F32), axis=1)
    ) / norm_gain
    return features_grad, query_grad, keyval_grad, output_grad, gain_grad


def solution(mesh):
    placed = (P("vrow", "vcol", None, "pix"), P("vrow", "vcol", None, "pix"), P(), P(), P(), P())
    return jax.shard_map(
        body,
        mesh=mesh,
        in_specs=placed,
        out_specs=(P("vrow", "vcol", None, "pix"), P(), P(), P(), P()),
        check_vma=False,
    )
```

```python
import functools
import math

import jax
import jax.numpy as jnp
from jax import lax
from jax.experimental import pallas as pl
from jax.experimental.pallas import tpu as pltpu
from jax.sharding import PartitionSpec as P


AXES = ("vrow", "vcol", "px", "py", "pc")
HEADS = 4
SIZE = 16
CH = 64
ROWS = 8
COLS = 2
PIX = 128
S = 13
EPSILON = 1e-06
SCALE = SIZE ** (-0.5)
F32 = jnp.float32
BF16 = jnp.bfloat16

VM = pl.BlockSpec(memory_space=pltpu.VMEM)
FAR = pl.BlockSpec(memory_space=pltpu.HBM)
SM = pl.BlockSpec(memory_space=pltpu.SMEM)


def inv_rms(values):
    return lax.rsqrt(jnp.mean(values * values, axis=0, keepdims=True) + EPSILON)


def total(terms):
    terms = list(terms)
    while len(terms) > 1:
        terms = [a + b for a, b in zip(terms[::2], terms[1::2])] + (
            [terms[-1]] if len(terms) % 2 else []
        )
    return terms[0]


def normed_pair(ref, row, gain):
    out = []
    for j in range(2):
        values = ref[row, j, 0:CH].astype(F32)
        out.append((values * inv_rms(values) * gain).astype(BF16))
    return jnp.concatenate(out, axis=1)


def put(ref, col, row, values):
    ref[col, pl.ds(row, values.shape[0], stride=S), :] = values


def take(ref, col, start):
    return ref[col, pl.ds(start, ROWS), :]


def row_pair(ref, row, first=0):
    return jnp.concatenate(
        [ref[row, 0, first : first + CH], ref[row, 1, first : first + CH]], axis=1
    )


def each_row(count, visits):
    def one(row, carry):
        for visit in visits:
            visit(row)
        return carry

    lax.fori_loop(0, count, one, 0)


def halo_start(side_ref):
    side = side_ref[0]
    return 10 - 10 * side, 10 * side, 6 - 6 * side


def clear_rows(refs, row):
    for ref in refs:
        zeros = jnp.zeros((ref.shape[1] // S, PIX), F32)
        for col in range(6):
            put(ref, col, row, zeros)
            put(ref, col, row + 1, zeros)


def project_views(ref, row, to_row, col, gain_full, w_full, qs, ks, vs, scales=None):
    raw = jnp.dot(w_full, normed_pair(ref, row, gain_full), preferred_element_type=F32)
    for j in range(2):
        part = raw[:, j * PIX : (j + 1) * PIX]
        query, key, value = part[:CH], part[CH : 2 * CH], part[2 * CH :]
        query_scale, key_scale = inv_rms(query), inv_rms(key)
        put(qs, col + j, to_row, (query * query_scale).astype(BF16).astype(F32))
        put(ks, col + j, to_row, (key * key_scale).astype(BF16).astype(F32))
        put(vs, col + j, to_row, value.astype(BF16).astype(F32))
        if scales is not None:
            scales[0][j, pl.ds(row, 1), :] = query_scale
            scales[1][j, pl.ds(row, 1), :] = key_scale


def project_out(both, to_row, col, w_o, ogs):
    og = jnp.dot(w_o, both, preferred_element_type=F32)
    for j in range(2):
        put(ogs, col + j, to_row, og[:, j * PIX : (j + 1) * PIX])


def eye():
    shape = (CH, CH)
    return lax.broadcasted_iota(jnp.int32, shape, 0) == lax.broadcasted_iota(jnp.int32, shape, 1)


def edge_kernel(side, feats, cot, edge, sems):
    _, _, edge_row = halo_start(side)
    copies = [
        pltpu.make_async_copy(
            source.at[pl.ds(edge_row, 2)], edge.at[:, :, k * CH : (k + 1) * CH], sems.at[k]
        )
        for k, source in enumerate((feats, cot))
    ]
    for copy in copies:
        copy.start()
    for copy in copies:
        copy.wait()


def own_kernel(
    side, feats_hbm, cot_hbm, gain, w_q_hbm, w_kv_hbm, w_out_hbm,
    qs, ks, vs, ogs, q_inv, k_inv, gain_out, w_in, w_back, feats, cot, w_q, w_kv, w_out, gain_row, sems,
):
    moves = (
        (gain, gain_row), (w_q_hbm, w_q), (w_kv_hbm, w_kv), (w_out_hbm, w_out),
        (feats_hbm, feats), (cot_hbm, cot),
    )
    copies = [pltpu.make_async_copy(a, b, sems.at[k]) for k, (a, b) in enumerate(moves)]
    for copy in copies:
        copy.start()
    _, clear_row, _ = halo_start(side)
    clear_rows((qs, ks, vs, ogs), clear_row)
    for copy in copies[:4]:
        copy.wait()
    gain_col = jnp.sum(
        jnp.where(eye(), jnp.broadcast_to(gain_row[...], (CH, CH)), 0.0), axis=1, keepdims=True
    )
    gain_full = jnp.broadcast_to(gain_col, (CH, PIX))
    gain_out[...] = gain_full
    w_in[0:CH, :] = w_q[...].astype(F32).T.astype(BF16)
    w_in[CH:, :] = w_kv[...].astype(F32).T.astype(BF16)
    w_back[...] = jnp.concatenate([w_q[...].astype(F32), w_kv[...].astype(F32)], axis=1).astype(BF16)
    w_full = w_in[...]
    w_o = w_out[...]
    for copy in copies[4:]:
        copy.wait()

    def visit(row):
        project_views(feats, row, row + 2, 2, gain_full, w_full, qs, ks, vs, (q_inv, k_inv))
        project_out(row_pair(cot, row), row + 2, 2, w_o, ogs)

    each_row(ROWS, (visit,))


def forward_kernel(
    side, left, right, row_halo, left_corner, right_corner, gain, w_in, ogs, qs_in, ks_in, vs_in,
    qs, ks, vs, weights, prob_grads, attended, stats, stats_edge,
):
    halo_row, _, edge_row = halo_start(side)
    gain_full = gain[...]
    w_full = w_in[...]

    def piece(ref, offset, col):
        return lambda row: project_views(ref, row, row + offset, col, gain_full, w_full, qs, ks, vs)

    each_row(ROWS, (piece(left, 2, 0), piece(right, 2, 4)))
    each_row(
        2, (piece(row_halo, halo_row, 2), piece(left_corner, halo_row, 0), piece(right_corner, halo_row, 4))
    )

    def attend(step, carry):
        col, head = step // HEADS, step % HEADS
        base = head * (SIZE * S)
        query = [take(qs, col + 2, base + d * S + 2) * SCALE for d in range(SIZE)]
        og = [take(ogs, col + 2, base + d * S + 2) for d in range(SIZE)]
        acc = [jnp.zeros((ROWS, PIX), F32)] * SIZE
        exp_total = jnp.zeros((ROWS, PIX), F32)
        spread = jnp.zeros((ROWS, PIX), F32)
        for j in range(5):
            for i in range(5):
                key = [take(ks, col + j, base + d * S + i) for d in range(SIZE)]
                weight = jnp.exp(total(a * b for a, b in zip(query, key)))
                value = [take(vs, col + j, base + d * S + i) for d in range(SIZE)]
                prob_grad = total(a * b for a, b in zip(og, value))
                acc = [a + weight * b for a, b in zip(acc, value)]
                exp_total = exp_total + weight
                spread = spread + weight * prob_grad
                weights[step, 5 * j + i] = weight
                prob_grads[step, 5 * j + i] = prob_grad
        inv_total = 1.0 / exp_total
        for d in range(SIZE):
            attended[col, pl.ds(pl.multiple_of((head * SIZE + d) * ROWS, ROWS), ROWS), :] = (
                acc[d] * inv_total
            )
        stats[pl.ds(col * 8 + head, ROWS, stride=16), :] = inv_total
        stats[pl.ds(col * 8 + 4 + head, ROWS, stride=16), :] = spread * inv_total
        return carry

    lax.fori_loop(0, COLS * HEADS, attend, 0)
    stats_edge[...] = stats[pl.ds(pl.multiple_of(edge_row * 16, 16), 32), :]


def unit_back(unit, scale, upstream):
    mean = jnp.sum(upstream * unit, axis=0, keepdims=True) * (1.0 / CH)
    return scale[None] * (upstream - unit * mean)


def own_channels(ref, col):
    return jnp.stack([take(ref, col + 2, d * S + 2) for d in range(CH)], axis=0)


def query_kernel(qs, ks, weights, prob_grads, stats, attended, cot, q_inv, raw_query, out_part, grads):
    def query_one(step, carry):
        col, head = step // HEADS, step % HEADS
        base = head * (SIZE * S)
        inv_total = stats[pl.ds(col * 8 + head, ROWS, stride=16), :]
        spread = stats[pl.ds(col * 8 + 4 + head, ROWS, stride=16), :]
        inv_total = inv_total * SCALE
        acc = [jnp.zeros((ROWS, PIX), F32)] * SIZE
        for j in range(5):
            for i in range(5):
                o = 5 * j + i
                score_grad = weights[step, o] * inv_total * (prob_grads[step, o] - spread)
                acc = [a + score_grad * take(ks, col + j, base + d * S + i) for d, a in enumerate(acc)]
        for d in range(SIZE):
            grads[col, head * SIZE + d] = acc[d]
        return carry

    lax.fori_loop(0, COLS * HEADS, query_one, 0)

    def finish(col, carry):
        raw = unit_back(own_channels(qs, col), q_inv[col], grads[col])
        raw_query[col] = raw.reshape(CH * ROWS, PIX)
        return carry

    lax.fori_loop(0, COLS, finish, 0)

    def out_grads(row, acc):
        mixed = [attended[j, pl.ds(row, CH, stride=ROWS), :].astype(BF16) for j in range(2)]
        return acc + lax.dot_general(
            jnp.concatenate(mixed, axis=1),
            row_pair(cot, row),
            (((1,), (1,)), ((), ())),
            preferred_element_type=F32,
        )

    out_part[...] = lax.fori_loop(0, ROWS, out_grads, jnp.zeros((CH, CH), F32))


def key_loop(view_cols, qs, ks, vs, ogs, sts, first, store):
    def key_one(step, carry):
        col, head = step // HEADS, step % HEADS
        base = head * (SIZE * S)
        key_acc, value_acc = first(col, head)
        for view_col in view_cols(col):
            for i in range(5):
                query = [take(qs, view_col, base + d * S + i) for d in range(SIZE)]
                key = [take(ks, col + 2, base + d * S + 2) for d in range(SIZE)]
                inv_total = take(sts, view_col, head * S + i)
                spread = take(sts, view_col, (head + HEADS) * S + i)
                score = total(a * b for a, b in zip(query, key))
                prob = jnp.exp(score * SCALE) * inv_total
                og = [take(ogs, view_col, base + d * S + i) for d in range(SIZE)]
                value = [take(vs, col + 2, base + d * S + 2) for d in range(SIZE)]
                prob_grad = total(a * b for a, b in zip(og, value))
                score_grad = prob * (prob_grad - spread)
                key_acc = [a + score_grad * b for a, b in zip(key_acc, query)]
                value_acc = [a + prob * b for a, b in zip(value_acc, og)]
        store(col, head, key_acc, value_acc)
        return carry

    lax.fori_loop(0, COLS * HEADS, key_one, 0)


def own_key_kernel(
    side, qs, ks, vs, stats, row_st, left, right, row_halo, left_corner, right_corner, w_out, ogs_in,
    ogs, key_grads, value_grads, sts,
):
    halo_row, clear_row, _ = halo_start(side)
    clear_rows((sts,), clear_row)
    w_o = w_out[...]

    def piece(ref, offset, col, first):
        return lambda row: project_out(row_pair(ref, row, first), row + offset, col, w_o, ogs)

    each_row(ROWS, (piece(left, 2, 0, 0), piece(right, 2, 4, 0)))
    each_row(
        2,
        (
            piece(row_halo, halo_row, 2, CH),
            piece(left_corner, halo_row, 0, CH),
            piece(right_corner, halo_row, 4, CH),
        ),
    )

    def own_stats(row):
        for j in range(2):
            put(sts, 2 + j, row + 2, stats[row, j])

    def halo_stats(row):
        for j in range(2):
            put(sts, 2 + j, row + halo_row, row_st[row, j])

    each_row(ROWS, (own_stats,))
    each_row(2, (halo_stats,))

    def first(col, head):
        zeros = [jnp.zeros((ROWS, PIX), F32)] * SIZE
        return zeros, zeros

    def store(col, head, key_acc, value_acc):
        for d in range(SIZE):
            key_grads[col, head * SIZE + d] = key_acc[d]
            value_grads[col, head * SIZE + d] = value_acc[d]

    key_loop(lambda col: (2, 3), qs, ks, vs, ogs, sts, first, store)


def key_kernel(
    side, qs, ks, vs, ogs, k_inv, raw_query, out_part, key_grads, value_grads,
    left_st, right_st, feats, cot, gain, w_back,
    feats_grad, weight_sums,
    sts, grads, raws,
):
    halo_row, clear_row, _ = halo_start(side)
    clear_rows((sts,), clear_row)

    def halo_stats(ref, offset, first, col):
        def one(row):
            for j in range(2):
                put(sts, col + j, row + offset, ref[row + first, j])

        return one

    each_row(ROWS, (halo_stats(left_st, 2, 0, 0), halo_stats(right_st, 2, 0, 4)))
    each_row(2, (halo_stats(left_st, halo_row, ROWS, 0), halo_stats(right_st, halo_row, ROWS, 4)))

    def first(col, head):
        return (
            [key_grads[col, head * SIZE + d] for d in range(SIZE)],
            [value_grads[col, head * SIZE + d] for d in range(SIZE)],
        )

    def store(col, head, key_acc, value_acc):
        for d in range(SIZE):
            grads[col, head * SIZE + d] = key_acc[d] * SCALE
            raws[col, pl.ds(pl.multiple_of((2 * CH + head * SIZE + d) * ROWS, ROWS), ROWS), :] = (
                value_acc[d]
            )

    key_loop(lambda col: (5 * col, 1, 4), qs, ks, vs, ogs, sts, first, store)

    def finish(col, carry):
        raw = unit_back(own_channels(ks, col), k_inv[col], grads[col])
        raws[col, CH * ROWS : 2 * CH * ROWS, :] = raw.reshape(CH * ROWS, PIX)
        raws[col, 0 : CH * ROWS, :] = raw_query[col]
        return carry

    lax.fori_loop(0, COLS, finish, 0)

    gain_full = gain[...]
    w_b = w_back[...]

    def view_row(row, acc):
        raw = jnp.concatenate(
            [raws[j, pl.ds(row, 3 * CH, stride=ROWS), :].astype(BF16) for j in range(2)], axis=1
        )
        normed_grad = jnp.dot(w_b, raw, preferred_element_type=F32)
        normed = []
        for j in range(2):
            values = feats[row, j].astype(F32)
            inv_norm = inv_rms(values)
            scaled = values * inv_norm
            normed.append((scaled * gain_full).astype(BF16))
            scaled_grad = normed_grad[:, j * PIX : (j + 1) * PIX] * gain_full
            mean = jnp.mean(scaled_grad * scaled, axis=0, keepdims=True)
            branch = inv_norm * (scaled_grad - scaled * mean)
            feats_grad[row, j] = (cot[row, j].astype(F32) + branch).astype(BF16)
        return acc + lax.dot_general(
            jnp.concatenate(normed, axis=1),
            raw,
            (((1,), (1,)), ((), ())),
            preferred_element_type=F32,
        )

    sums = lax.fori_loop(0, ROWS, view_row, jnp.zeros((CH, 3 * CH), F32))
    weight_sums[0:CH, :] = sums[:, CH:]
    weight_sums[CH : 2 * CH, :] = jnp.concatenate([sums[:, :CH], out_part[...]], axis=1)


def last_kernel(factor, sums, w_q, w_kv, gain, query_grad, keyval_grad, output_grad, gain_grad):
    keyval = sums[0:CH, :] * factor
    rest = sums[CH : 2 * CH, :] * factor
    query = rest[:, :CH]
    keyval_grad[...] = keyval
    query_grad[...] = query
    output_grad[...] = rest[:, CH:]
    col = jnp.sum(query * w_q[...].astype(F32), axis=1, keepdims=True) + jnp.sum(
        keyval * w_kv[...].astype(F32), axis=1, keepdims=True
    )
    line = jnp.sum(jnp.where(eye(), jnp.broadcast_to(col, (CH, CH)), 0.0), axis=0, keepdims=True)
    gain_grad[...] = line / gain[...]


def call(kernel, outs, scratch, flops, *operands, aliases=(), far=()):
    return pl.pallas_call(
        kernel,
        out_shape=[jax.ShapeDtypeStruct(shape, dtype) for shape, dtype in outs],
        in_specs=[
            SM if x.dtype == jnp.int32 else FAR if k in far else VM for k, x in enumerate(operands)
        ],
        out_specs=[VM] * len(outs),
        scratch_shapes=[pltpu.VMEM(x, F32) if isinstance(x, tuple) else x for x in scratch],
        input_output_aliases=dict(aliases),
        compiler_params=pltpu.CompilerParams(vmem_limit_bytes=32 * 1024 * 1024),
        cost_estimate=pl.CostEstimate(flops=flops, bytes_accessed=1000000, transcendentals=0),
    )(*operands)


def sum_everywhere(values):
    near, far = ("px", "pc", "vrow"), ("py", "vcol")
    near_count, far_count = (math.prod(lax.axis_size(a) for a in axes) for axes in (near, far))
    shares = lax.all_to_all(values.reshape(near_count, -1, PIX), near, 0, 0)
    share = jnp.sum(shares, axis=0).astype(BF16)
    copies = jnp.broadcast_to(share[None], (far_count,) + share.shape)
    share = jnp.sum(lax.all_to_all(copies, far, 0, 0).astype(F32), axis=0)
    copies = jnp.broadcast_to(share[None], (near_count,) + share.shape)
    return lax.all_to_all(copies, near, 0, 0).reshape(values.shape)


def layer(features, out_cotangent, norm_gain, query_proj, keyval_proj, output_proj):
    vrow = lax.axis_index("vrow").astype(jnp.int32)
    side = vrow.reshape(1)
    cols = lax.axis_size("vcol")
    up = [(i, i + 1) for i in range(cols - 1)]
    down = [(j, i) for i, j in up]
    cross = [(0, 1), (1, 0)]
    diag_up = [(a * cols + i, b * cols + j) for a, b in cross for i, j in up]
    diag_down = [(a * cols + i, b * cols + j) for a, b in cross for i, j in down]
    grid = ("vrow", "vcol")

    held = [pltpu.with_memory_space_constraint(x, pltpu.HBM) for x in (features, out_cotangent)]
    left = lax.ppermute(features, "vcol", up)
    right = lax.ppermute(features, "vcol", down)
    (edge,) = call(
        edge_kernel,
        [((2, COLS, 2 * CH, PIX), BF16)],
        [pltpu.SemaphoreType.DMA((2,))], 1000,
        side, *held, far=(1, 2),
    )
    row_halo = lax.ppermute(edge, "vrow", cross)
    left_corner = lax.ppermute(edge, grid, diag_up)
    right_corner = lax.ppermute(edge, grid, diag_down)

    padded = ((6, CH * S, PIX), F32)
    lanes = ((COLS, ROWS, PIX), F32)
    offsets = ((COLS * HEADS, 25, ROWS, PIX), F32)
    channels = ((COLS, CH * ROWS, PIX), F32)
    tiles = ((COLS, CH, ROWS, PIX), F32)
    gain = norm_gain.reshape(1, CH)
    views = (features.shape, BF16)
    (
        qs, ks, vs, ogs, q_inv, k_inv, gain_full, w_in, w_back, feats, cot, w_q, w_kv, w_out, gain_row,
    ) = call(
        own_kernel,
        [
            padded, padded, padded, padded, lanes, lanes, ((CH, PIX), F32), ((3 * CH, CH), BF16),
            ((CH, 3 * CH), BF16), views, views, ((CH, CH), BF16), ((CH, 2 * CH), BF16),
            ((CH, CH), BF16), ((1, CH), F32),
        ],
        [pltpu.SemaphoreType.DMA((6,))], 2000000,
        side, *held, *(pltpu.with_memory_space_constraint(x, pltpu.HBM) for x in (gain, query_proj, keyval_proj, output_proj)),
        far=(1, 2, 3, 4, 5, 6),
    )
    left_cot = lax.ppermute(out_cotangent, "vcol", up)
    right_cot = lax.ppermute(out_cotangent, "vcol", down)
    qs, ks, vs, weights, prob_grads, attended, stats, stats_edge = call(
        forward_kernel,
        [padded, padded, padded, offsets, offsets, channels, ((ROWS * 16, PIX), F32), ((32, PIX), F32)],
        [], 4000000,
        side, left, right, row_halo, left_corner, right_corner, gain_full, w_in, ogs, qs, ks, vs,
        aliases=((9, 0), (10, 1), (11, 2)),
    )
    stats_view = stats.reshape(ROWS, COLS, 8, PIX)
    row_st = lax.ppermute(stats_edge.reshape(2, COLS, 8, PIX), "vrow", cross)
    raw_query, out_part = call(
        query_kernel,
        [channels, ((CH, CH), F32)],
        [(COLS, CH, ROWS, PIX)], 2000000,
        qs, ks, weights, prob_grads, stats, attended, cot, q_inv,
    )
    all_st = jnp.concatenate([stats_view, row_st], axis=0)
    left_st = lax.ppermute(all_st, "vcol", up)
    right_st = lax.ppermute(all_st, "vcol", down)
    ogs, key_grads, value_grads = call(
        own_key_kernel,
        [padded, tiles, tiles],
        [(6, 8 * S, PIX)], 3000000,
        side, qs, ks, vs, stats_view, row_st,
        left_cot, right_cot, row_halo, left_corner, right_corner, w_out, ogs,
        aliases=((12, 0),),
    )
    features_grad, weight_sums = call(
        key_kernel,
        [(features.shape, BF16), ((2 * CH, PIX), F32)],
        [(6, 8 * S, PIX), (COLS, CH, ROWS, PIX), (COLS, 3 * CH * ROWS, PIX)], 4000000,
        side, qs, ks, vs, ogs, k_inv, raw_query, out_part, key_grads, value_grads,
        left_st, right_st, feats, cot, gain_full, w_back,
    )
    tokens_all = ROWS * COLS * PIX * math.prod(lax.axis_size(a) for a in AXES)
    query_grad, keyval_grad, output_grad, gain_grad = call(
        functools.partial(last_kernel, 1.0 / math.sqrt(tokens_all)),
        [((CH, CH), F32), ((CH, 2 * CH), F32), ((CH, CH), F32), ((1, CH), F32)],
        [], 100000,
        sum_everywhere(weight_sums), w_q, w_kv, gain_row,
    )
    return features_grad, query_grad, keyval_grad, output_grad, gain_grad.reshape(CH)


def solution(mesh):
    rows, cols, _ = mesh.devices.shape
    parts = jax.sharding.Mesh(mesh.devices.reshape(rows, cols, 4, 4, 2), AXES)
    placed = P("vrow", "vcol", None, AXES[2:])
    return jax.shard_map(
        layer,
        mesh=parts,
        in_specs=(placed, placed, P(), P(), P(), P()),
        out_specs=(placed, P(), P(), P(), P()),
        check_vma=False,
    )
```

```python
import functools
import math

import jax
import jax.numpy as jnp
from jax import lax
from jax.experimental import pallas as pl
from jax.experimental.pallas import tpu as pltpu
from jax.sharding import PartitionSpec as P


AXES = ("vrow", "vcol", "px", "py", "pc")
HEADS = 4
SIZE = 16
CH = 64
ROWS = 8
COLS = 2
PIX = 128
S = 13
W = 13
EPSILON = 1e-06
SCALE = SIZE ** (-0.5)
F32 = jnp.float32
BF16 = jnp.bfloat16

VM = pl.BlockSpec(memory_space=pltpu.VMEM)
FAR = pl.BlockSpec(memory_space=pltpu.HBM)
SM = pl.BlockSpec(memory_space=pltpu.SMEM)


def inv_rms(values):
    return lax.rsqrt(jnp.mean(values * values, axis=0, keepdims=True) + EPSILON)


def total(terms):
    terms = list(terms)
    while len(terms) > 1:
        terms = [a + b for a, b in zip(terms[::2], terms[1::2])] + (
            [terms[-1]] if len(terms) % 2 else []
        )
    return terms[0]


def put(ref, col, row, values):
    ref[col, pl.ds(row, values.shape[0], stride=S), :] = values


def take(ref, col, start):
    return ref[col, pl.ds(start, ROWS), :]


def pair(ref, row, first=0):
    return jnp.concatenate([ref[row, first], ref[row, first + 1]], axis=1)


def each_row(count, visits):
    def one(row, carry):
        for visit in visits:
            visit(row)
        return carry

    lax.fori_loop(0, count, one, 0)


def halo_start(side_ref):
    side = side_ref[0]
    return 10 - 10 * side, 10 * side, 6 - 6 * side


def clear_rows(refs, row):
    for ref in refs:
        zeros = jnp.zeros((ref.shape[1] // S, PIX), F32)
        for col in range(ref.shape[0]):
            put(ref, col, row, zeros)
            put(ref, col, row + 1, zeros)


def eye():
    shape = (CH, CH)
    return lax.broadcasted_iota(jnp.int32, shape, 0) == lax.broadcasted_iota(jnp.int32, shape, 1)


def normed_views(ref, row, gain):
    out = []
    for j in range(2):
        values = ref[row, j].astype(F32)
        out.append((values * inv_rms(values) * gain).astype(BF16))
    return out


def project_keys(raw, to_row, col, j, ks, vs, k_inv):
    key, value = raw[:CH], raw[CH:]
    key_scale = inv_rms(key)
    put(ks, col + j, to_row, (key * key_scale).astype(BF16).astype(F32))
    put(vs, col + j, to_row, value.astype(BF16).astype(F32))
    k_inv[col + j, pl.ds(to_row, 1), :] = key_scale


def edge_kernel(side, feats, edge, sem):
    _, _, edge_row = halo_start(side)
    copy = pltpu.make_async_copy(feats.at[pl.ds(edge_row, 2)], edge, sem)
    copy.start()
    copy.wait()


def own_kernel(
    side, feats_hbm, cot_hbm, gain_hbm, w_q_hbm, w_kv_hbm, w_out_hbm,
    qs, ks, vs, ogs, q_inv, k_inv, normed, gain_out, w_in, w_back, feats, cot, w_q, w_kv, gain_row,
    w_out, sems,
):
    moves = (
        (gain_hbm, gain_row), (w_q_hbm, w_q), (w_kv_hbm, w_kv), (w_out_hbm, w_out),
        (feats_hbm, feats), (cot_hbm, cot),
    )
    copies = [pltpu.make_async_copy(a, b, sems.at[k]) for k, (a, b) in enumerate(moves)]
    for copy in copies:
        copy.start()
    _, clear_row, _ = halo_start(side)
    clear_rows((ks, vs), clear_row)
    clear_rows((qs, ogs), 0)
    clear_rows((qs, ogs), 10)
    for copy in copies[:4]:
        copy.wait()
    gain_col = jnp.sum(
        jnp.where(eye(), jnp.broadcast_to(gain_row[...], (CH, CH)), 0.0), axis=1, keepdims=True
    )
    gain_full = jnp.broadcast_to(gain_col, (CH, PIX))
    gain_out[...] = gain_full
    w_in[0:CH, :] = w_q[...].astype(F32).T.astype(BF16)
    w_in[CH:, :] = w_kv[...].astype(F32).T.astype(BF16)
    w_back[...] = jnp.concatenate([w_q[...].astype(F32), w_kv[...].astype(F32)], axis=1).astype(BF16)
    w_full = w_in[...]
    w_o = w_out[...]
    for copy in copies[4:]:
        copy.wait()

    def visit(row):
        views = normed_views(feats, row, gain_full)
        both = jnp.dot(w_full, jnp.concatenate(views, axis=1), preferred_element_type=F32)
        out_both = jnp.dot(w_o, pair(cot, row), preferred_element_type=F32)
        for j in range(2):
            normed[row, 2 + j] = views[j]
            raw = both[:, j * PIX : (j + 1) * PIX]
            query_scale = inv_rms(raw[:CH])
            put(qs, j, row + 2, (raw[:CH] * query_scale).astype(BF16).astype(F32))
            q_inv[j, pl.ds(row, 1), :] = query_scale
            project_keys(raw[CH:], row + 2, 2, j, ks, vs, k_inv)
            put(ogs, j, row + 2, out_both[:, j * PIX : (j + 1) * PIX])

    each_row(ROWS, (visit,))


def forward_kernel(
    side, left, right, row_halo, left_corner, right_corner, gain, w_in, ogs, qs,
    ks_in, vs_in, k_inv_in, normed_in,
    ks, vs, k_inv, normed, weights, prob_grads, attended, stats,
):
    halo_row, _, _ = halo_start(side)
    gain_full = gain[...]
    w_keys = w_in[CH:, :]

    def piece(ref, offset, first, col):
        def one(row):
            views = normed_views(ref, row, gain_full)
            both = jnp.dot(w_keys, jnp.concatenate(views, axis=1), preferred_element_type=F32)
            for j in range(2):
                normed[row + first, col + j] = views[j]
                project_keys(both[:, j * PIX : (j + 1) * PIX], row + offset, col, j, ks, vs, k_inv)

        return one

    each_row(ROWS, (piece(left, 2, 0, 0), piece(right, 2, 0, 4)))
    each_row(
        2,
        (
            piece(row_halo, halo_row, ROWS, 2),
            piece(left_corner, halo_row, ROWS, 0),
            piece(right_corner, halo_row, ROWS, 4),
        ),
    )

    def attend(step, carry):
        col, head = step // HEADS, step % HEADS
        base = head * (SIZE * S)
        query = [take(qs, col, base + d * S + 2) * SCALE for d in range(SIZE)]
        og = [take(ogs, col, base + d * S + 2) for d in range(SIZE)]
        acc = [jnp.zeros((ROWS, PIX), F32)] * SIZE
        exp_total = jnp.zeros((ROWS, PIX), F32)
        spread = jnp.zeros((ROWS, PIX), F32)
        for j in range(5):
            for i in range(5):
                key = [take(ks, col + j, base + d * S + i) for d in range(SIZE)]
                weight = jnp.exp(total(a * b for a, b in zip(query, key)))
                value = [take(vs, col + j, base + d * S + i) for d in range(SIZE)]
                prob_grad = total(a * b for a, b in zip(og, value))
                acc = [a + weight * b for a, b in zip(acc, value)]
                exp_total = exp_total + weight
                spread = spread + weight * prob_grad
                weights[step, 5 * j + i] = weight
                prob_grads[step, 5 * j + i] = prob_grad
        inv_total = 1.0 / exp_total
        for d in range(SIZE):
            attended[col, pl.ds(pl.multiple_of((head * SIZE + d) * ROWS, ROWS), ROWS), :] = (
                acc[d] * inv_total
            )
        stats[0, step] = inv_total
        stats[1, step] = spread * inv_total
        return carry

    lax.fori_loop(0, COLS * HEADS, attend, 0)


def unit_back(unit, scale, upstream):
    mean = jnp.sum(upstream * unit, axis=0, keepdims=True) * (1.0 / CH)
    return scale[None] * (upstream - unit * mean)


def window(ref, col, row):
    return jnp.stack([take(ref, col, d * S + row) for d in range(CH)], axis=0)


def outer(left, right):
    return lax.dot_general(left, right, (((1,), (1,)), ((), ())), preferred_element_type=F32)


def gradient_kernel(
    side, qs, ks, ogs, q_inv, k_inv, normed, weights, prob_grads, attended, stats, cot,
    weight_sums, raw_query, to_left, to_right, own_raw,
    probs, score_grads, grads, raws, halo_grads, halo_raws,
):
    _, _, edge_row = halo_start(side)
    zeros = jnp.zeros((ROWS, PIX), F32)

    def query_one(step, carry):
        col, head = step // HEADS, step % HEADS
        base = head * (SIZE * S)
        inv_total, spread = stats[0, step], stats[1, step]
        acc = [zeros] * SIZE
        for j in range(5):
            for i in range(5):
                o = 5 * j + i
                prob = weights[step, o] * inv_total
                score_grad = prob * (prob_grads[step, o] - spread) * SCALE
                for ref, values in ((probs, prob), (score_grads, score_grad)):
                    ref[step, pl.ds(o * W, 2), :] = zeros[:2]
                    ref[step, pl.ds(o * W + 2, ROWS), :] = values
                    ref[step, pl.ds(o * W + 10, 2), :] = zeros[:2]
                acc = [a + score_grad * take(ks, col + j, base + d * S + i) for d, a in enumerate(acc)]
        for d in range(SIZE):
            grads[0, head * SIZE + d + col * CH] = acc[d]
        return carry

    lax.fori_loop(0, COLS * HEADS, query_one, 0)

    def query_finish(col, carry):
        first = pl.multiple_of(col * CH, CH)
        raw = unit_back(window(qs, col, 2), q_inv[col], grads[0, pl.ds(first, CH)])
        raws[col, 0 : CH * ROWS, :] = raw.reshape(CH * ROWS, PIX)
        return carry

    lax.fori_loop(0, COLS, query_finish, 0)

    def query_sums(row, carry):
        query_acc, out_acc = carry
        raw = [raws[j, pl.ds(row, CH, stride=ROWS), :].astype(BF16) for j in range(2)]
        mixed = [attended[j, pl.ds(row, CH, stride=ROWS), :].astype(BF16) for j in range(2)]
        for j in range(2):
            raw_query[row, j] = raw[j]
        return (
            query_acc + outer(pair(normed, row, 2), jnp.concatenate(raw, axis=1)),
            out_acc + outer(jnp.concatenate(mixed, axis=1), pair(cot, row)),
        )

    flat = jnp.zeros((CH, CH), F32)
    query_acc, out_acc = lax.fori_loop(0, ROWS, query_sums, (flat, flat))
    weight_sums[CH : 2 * CH, :] = jnp.concatenate([query_acc, out_acc], axis=1)

    def key_step(acc, step, col, j, i, base, first_row):
        key_acc, value_acc = acc
        start = first_row - i + 2
        prob = probs[step, pl.ds((5 * j + i) * W + start, ROWS), :]
        score_grad = score_grads[step, pl.ds((5 * j + i) * W + start, ROWS), :]
        key_acc = [a + score_grad * take(qs, col, base + d * S + start) for d, a in enumerate(key_acc)]
        value_acc = [a + prob * take(ogs, col, base + d * S + start) for d, a in enumerate(value_acc)]
        return key_acc, value_acc

    edge_first, edge_offset = edge_row * 2 // 3, edge_row // 2

    def key_columns(view_col, head, cols):
        base = head * (SIZE * S)
        acc = ([zeros] * SIZE, [zeros] * SIZE)
        for col in cols:
            for i in range(5):
                acc = key_step(acc, col * HEADS + head, col, view_col - col, i, base, 2)
        for d in range(SIZE):
            grads[view_col, head * SIZE + d] = acc[0][d]
            grads[view_col, CH + head * SIZE + d] = acc[1][d]
        acc = ([zeros] * SIZE, [zeros] * SIZE)
        for col in cols:
            for i in range(2):
                acc = key_step(
                    acc, col * HEADS + head, col, view_col - col, edge_offset + i, base, edge_first
                )
        for d in range(SIZE):
            halo_grads[view_col, head * SIZE + d] = acc[0][d]
            halo_grads[view_col, CH + head * SIZE + d] = acc[1][d]

    def inner_columns(step, carry):
        key_columns(1 + step // HEADS, step % HEADS, (0, 1))
        return carry

    def outer_columns(step, carry):
        side_col = step // HEADS
        key_columns(5 * side_col, step % HEADS, (side_col,))
        return carry

    lax.fori_loop(0, 4 * HEADS, inner_columns, 0)
    lax.fori_loop(0, 2 * HEADS, outer_columns, 0)

    def key_finish(col, carry):
        for source, target, row in ((grads, raws, 2), (halo_grads, halo_raws, edge_first)):
            scale = k_inv[col, pl.ds(row, ROWS), :]
            raw = unit_back(window(ks, col, row), scale, source[col, 0:CH])
            target[col, 0 : CH * ROWS, :] = raw.reshape(CH * ROWS, PIX)
            target[col, CH * ROWS :, :] = source[col, CH:].reshape(CH * ROWS, PIX)
        return carry

    lax.fori_loop(0, 6, key_finish, 0)

    def key_sums(source, from_row, first):
        def one(row, acc):
            for col, target in ((0, to_left), (2, own_raw), (4, to_right)):
                raw = [
                    source[col + j, pl.ds(row + from_row, 2 * CH, stride=ROWS), :].astype(BF16)
                    for j in range(2)
                ]
                for j in range(2):
                    target[row + first, j] = raw[j]
                acc = acc + outer(pair(normed, row + first, col), jnp.concatenate(raw, axis=1))
            return acc

        return one

    acc = lax.fori_loop(0, ROWS, key_sums(raws, 0, 0), jnp.zeros((CH, 2 * CH), F32))
    weight_sums[0:CH, :] = lax.fori_loop(0, 2, key_sums(halo_raws, edge_row, ROWS), acc)


def features_kernel(
    side, own_raw, left_raw, right_raw, row_raw, raw_query, feats, cot, gain, w_back,
    feats_grad, shared,
):
    _, _, edge_row = halo_start(side)

    def join(row):
        for j in range(2):
            shared[row, j] = (
                own_raw[row, j].astype(F32) + left_raw[row, j].astype(F32)
                + right_raw[row, j].astype(F32)
            )

    def join_edge(row):
        for j in range(2):
            shared[row + edge_row, j] = shared[row + edge_row, j] + row_raw[row, j].astype(F32)

    each_row(ROWS, (join,))
    each_row(2, (join_edge,))
    gain_full = gain[...]
    w_b = w_back[...]

    def view_row(row):
        raw = jnp.concatenate([pair(raw_query, row), pair(shared, row).astype(BF16)], axis=0)
        normed_grad = jnp.dot(w_b, raw, preferred_element_type=F32)
        for j in range(2):
            values = feats[row, j].astype(F32)
            inv_norm = inv_rms(values)
            scaled = values * inv_norm
            scaled_grad = normed_grad[:, j * PIX : (j + 1) * PIX] * gain_full
            mean = jnp.mean(scaled_grad * scaled, axis=0, keepdims=True)
            branch = inv_norm * (scaled_grad - scaled * mean)
            feats_grad[row, j] = (cot[row, j].astype(F32) + branch).astype(BF16)

    each_row(ROWS, (view_row,))


def last_kernel(factor, sums, w_q, w_kv, gain, query_grad, keyval_grad, output_grad, gain_grad):
    keyval = sums[0:CH, :] * factor
    rest = sums[CH : 2 * CH, :] * factor
    query = rest[:, :CH]
    keyval_grad[...] = keyval
    query_grad[...] = query
    output_grad[...] = rest[:, CH:]
    col = jnp.sum(query * w_q[...].astype(F32), axis=1, keepdims=True) + jnp.sum(
        keyval * w_kv[...].astype(F32), axis=1, keepdims=True
    )
    line = jnp.sum(jnp.where(eye(), jnp.broadcast_to(col, (CH, CH)), 0.0), axis=0, keepdims=True)
    gain_grad[...] = line / gain[...]


def call(kernel, outs, scratch, flops, *operands, aliases=(), far=()):
    return pl.pallas_call(
        kernel,
        out_shape=[jax.ShapeDtypeStruct(shape, dtype) for shape, dtype in outs],
        in_specs=[
            SM if x.dtype == jnp.int32 else FAR if k in far else VM for k, x in enumerate(operands)
        ],
        out_specs=[VM] * len(outs),
        scratch_shapes=[pltpu.VMEM(x, F32) if isinstance(x, tuple) else x for x in scratch],
        input_output_aliases=dict(aliases),
        compiler_params=pltpu.CompilerParams(vmem_limit_bytes=32 * 1024 * 1024),
        cost_estimate=pl.CostEstimate(flops=flops, bytes_accessed=1000000, transcendentals=0),
    )(*operands)


def sum_everywhere(values):
    near, far = ("px", "pc", "vrow"), ("py", "vcol")
    near_count, far_count = (math.prod(lax.axis_size(a) for a in axes) for axes in (near, far))
    shares = lax.all_to_all(values.reshape(near_count, -1, PIX), near, 0, 0)
    share = jnp.sum(shares, axis=0).astype(BF16)
    copies = jnp.broadcast_to(share[None], (far_count,) + share.shape)
    shares = lax.all_to_all(copies, far, 0, 0)
    share = jnp.sum(shares.astype(F32), axis=0)
    copies = jnp.broadcast_to(share[None], (near_count,) + share.shape)
    return lax.all_to_all(copies, near, 0, 0).reshape(values.shape)


def layer(features, out_cotangent, norm_gain, query_proj, keyval_proj, output_proj):
    side = lax.axis_index("vrow").astype(jnp.int32).reshape(1)
    cols = lax.axis_size("vcol")
    up = [(i, i + 1) for i in range(cols - 1)]
    down = [(j, i) for i, j in up]
    cross = [(0, 1), (1, 0)]
    diag_up = [(a * cols + i, b * cols + j) for a, b in cross for i, j in up]
    diag_down = [(a * cols + i, b * cols + j) for a, b in cross for i, j in down]
    grid = ("vrow", "vcol")
    gain = norm_gain.reshape(1, CH)
    held = [
        pltpu.with_memory_space_constraint(x, pltpu.HBM)
        for x in (features, out_cotangent, gain, query_proj, keyval_proj, output_proj)
    ]

    left = lax.ppermute(features, "vcol", up)
    right = lax.ppermute(features, "vcol", down)
    (edge,) = call(
        edge_kernel, [((2, COLS, CH, PIX), BF16)], [pltpu.SemaphoreType.DMA], 1000, side, held[0],
        far=(1,),
    )
    row_halo = lax.ppermute(edge, "vrow", cross)
    left_corner = lax.ppermute(edge, grid, diag_up)
    right_corner = lax.ppermute(edge, grid, diag_down)

    own = ((COLS, CH * S, PIX), F32)
    padded = ((6, CH * S, PIX), F32)
    lanes = ((COLS, ROWS, PIX), F32)
    key_lanes = ((6, 16, PIX), F32)
    steps = COLS * HEADS
    offsets = ((steps, 25, ROWS, PIX), F32)
    views = ((ROWS, COLS, CH, PIX), BF16)
    all_views = ((ROWS + 2, 6, CH, PIX), BF16)
    key_views = ((ROWS + 2, COLS, 2 * CH, PIX), BF16)
    (
        qs, ks, vs, ogs, q_inv, k_inv, normed, gain_full, w_in, w_back, feats, cot, w_q, w_kv, gain_row,
    ) = call(
        own_kernel,
        [
            own, padded, padded, own, lanes, key_lanes, all_views, ((CH, PIX), F32),
            ((3 * CH, CH), BF16), ((CH, 3 * CH), BF16), views, views, ((CH, CH), BF16),
            ((CH, 2 * CH), BF16), ((1, CH), F32),
        ],
        [pltpu.VMEM((CH, CH), BF16), pltpu.SemaphoreType.DMA((6,))], 2000000,
        side, *held, far=(1, 2, 3, 4, 5, 6),
    )
    ks, vs, k_inv, normed, weights, prob_grads, attended, stats = call(
        forward_kernel,
        [
            padded, padded, key_lanes, all_views, offsets, offsets,
            ((COLS, CH * ROWS, PIX), F32), ((2, steps, ROWS, PIX), F32),
        ],
        [], 4000000,
        side, left, right, row_halo, left_corner, right_corner, gain_full, w_in, ogs, qs,
        ks, vs, k_inv, normed,
        aliases=((10, 0), (11, 1), (12, 2), (13, 3)),
    )
    weight_sums, raw_query, to_left, to_right, own_raw = call(
        gradient_kernel,
        [((2 * CH, PIX), F32), views, key_views, key_views, key_views],
        [
            (steps, 25 * W, PIX), (steps, 25 * W, PIX), (6, 2 * CH, ROWS, PIX),
            (6, 2 * CH * ROWS, PIX), (6, 2 * CH, ROWS, PIX), (6, 2 * CH * ROWS, PIX),
        ],
        5000000,
        side, qs, ks, ogs, q_inv, k_inv, normed, weights, prob_grads, attended, stats, cot,
    )
    sums = sum_everywhere(weight_sums)
    right_raw = lax.ppermute(to_left, "vcol", down)
    left_raw = lax.ppermute(to_right, "vcol", up)
    row_send = sum(x[ROWS:].astype(F32) for x in (own_raw, left_raw, right_raw)).astype(BF16)
    row_raw = lax.ppermute(row_send, "vrow", cross)
    (features_grad,) = call(
        features_kernel, [(features.shape, BF16)], [(ROWS, COLS, 2 * CH, PIX)], 2000000,
        side, own_raw, left_raw, right_raw, row_raw, raw_query, feats, cot, gain_full, w_back,
    )
    tokens_all = ROWS * COLS * PIX * math.prod(lax.axis_size(a) for a in AXES)
    query_grad, keyval_grad, output_grad, gain_grad = call(
        functools.partial(last_kernel, 1.0 / math.sqrt(tokens_all)),
        [((CH, CH), F32), ((CH, 2 * CH), F32), ((CH, CH), F32), ((1, CH), F32)],
        [], 100000,
        sums, w_q, w_kv, gain_row,
    )
    return features_grad, query_grad, keyval_grad, output_grad, gain_grad.reshape(CH)


def solution(mesh):
    rows, cols, _ = mesh.devices.shape
    parts = jax.sharding.Mesh(mesh.devices.reshape(rows, cols, 4, 4, 2), AXES)
    placed = P("vrow", "vcol", None, AXES[2:])
    return jax.shard_map(
        layer,
        mesh=parts,
        in_specs=(placed, placed, P(), P(), P(), P()),
        out_specs=(placed, P(), P(), P(), P()),
        check_vma=False,
    )
```

```python
import functools
import math

import jax
import jax.numpy as jnp
from jax import lax
from jax.experimental import pallas as pl
from jax.experimental.pallas import tpu as pltpu
from jax.sharding import PartitionSpec as P


AXES = ("vrow", "vcol", "px", "py", "pc")
HEADS = 4
SIZE = 16
CH = 64
ROWS = 8
COLS = 2
PIX = 128
S = 13
W = 13
R = 9
EPSILON = 1e-06
SCALE = SIZE ** (-0.5)
F32 = jnp.float32
BF16 = jnp.bfloat16

VM = pl.BlockSpec(memory_space=pltpu.VMEM)
FAR = pl.BlockSpec(memory_space=pltpu.HBM)
SM = pl.BlockSpec(memory_space=pltpu.SMEM)


def inv_rms(values):
    return lax.rsqrt(jnp.mean(values * values, axis=0, keepdims=True) + EPSILON)


def total(terms):
    terms = list(terms)
    while len(terms) > 1:
        terms = [a + b for a, b in zip(terms[::2], terms[1::2])] + (
            [terms[-1]] if len(terms) % 2 else []
        )
    return terms[0]


def put(ref, col, row, values):
    ref[col, pl.ds(row, values.shape[0], stride=S), :] = values


def take(ref, col, start):
    return ref[col, pl.ds(start, ROWS), :]


def pair(ref, row, first=0):
    return jnp.concatenate([ref[row, first], ref[row, first + 1]], axis=1)


def each_row(count, visits):
    def one(row, carry):
        for visit in visits:
            visit(row)
        return carry

    lax.fori_loop(0, count, one, 0)


def halo_start(side_ref):
    side = side_ref[0]
    return 10 - 10 * side, 10 * side, 6 - 6 * side


def clear_rows(refs, row):
    for ref in refs:
        zeros = jnp.zeros((ref.shape[1] // S, PIX), F32)
        for col in range(ref.shape[0]):
            put(ref, col, row, zeros)
            put(ref, col, row + 1, zeros)


def eye():
    shape = (CH, CH)
    return lax.broadcasted_iota(jnp.int32, shape, 0) == lax.broadcasted_iota(jnp.int32, shape, 1)


def normed_views(ref, row, gain):
    out = []
    for j in range(2):
        values = ref[row, j].astype(F32)
        out.append((values * inv_rms(values) * gain).astype(BF16))
    return out


def project_keys(raw, to_row, col, j, ks, vs, k_inv):
    key, value = raw[:CH], raw[CH:]
    key_scale = inv_rms(key)
    put(ks, col + j, to_row, (key * key_scale).astype(BF16).astype(F32))
    put(vs, col + j, to_row, value.astype(BF16).astype(F32))
    k_inv[col + j, pl.ds(to_row, 1), :] = key_scale


def edge_kernel(side, feats, edge, sem):
    _, _, edge_row = halo_start(side)
    copy = pltpu.make_async_copy(feats.at[pl.ds(edge_row, 2)], edge, sem)
    copy.start()
    copy.wait()


def own_kernel(
    side, feats_hbm, cot_hbm, gain_hbm, w_q_hbm, w_kv_hbm, w_out_hbm,
    qs, ks, vs, ogs, q_inv, k_inv, normed, gain_out, w_in, w_back, feats, cot, w_q, w_kv, gain_row,
    w_out, sems,
):
    moves = (
        (gain_hbm, gain_row), (w_q_hbm, w_q), (w_kv_hbm, w_kv), (w_out_hbm, w_out),
        (feats_hbm, feats), (cot_hbm, cot),
    )
    copies = [pltpu.make_async_copy(a, b, sems.at[k]) for k, (a, b) in enumerate(moves)]
    for copy in copies:
        copy.start()
    _, clear_row, _ = halo_start(side)
    clear_rows((ks, vs), clear_row)
    clear_rows((qs, ogs), 0)
    clear_rows((qs, ogs), 10)
    for copy in copies[:4]:
        copy.wait()
    gain_col = jnp.sum(
        jnp.where(eye(), jnp.broadcast_to(gain_row[...], (CH, CH)), 0.0), axis=1, keepdims=True
    )
    gain_full = jnp.broadcast_to(gain_col, (CH, PIX))
    gain_out[...] = gain_full
    w_in[0:CH, :] = w_q[...].astype(F32).T.astype(BF16)
    w_in[CH:, :] = w_kv[...].astype(F32).T.astype(BF16)
    w_back[...] = jnp.concatenate([w_q[...].astype(F32), w_kv[...].astype(F32)], axis=1).astype(BF16)
    w_full = w_in[...]
    w_o = w_out[...]
    for copy in copies[4:]:
        copy.wait()

    def visit(row):
        views = normed_views(feats, row, gain_full)
        both = jnp.dot(w_full, jnp.concatenate(views, axis=1), preferred_element_type=F32)
        out_both = jnp.dot(w_o, pair(cot, row), preferred_element_type=F32)
        for j in range(2):
            normed[row, 2 + j] = views[j]
            raw = both[:, j * PIX : (j + 1) * PIX]
            query_scale = inv_rms(raw[:CH])
            put(qs, j, row + 2, (raw[:CH] * query_scale).astype(BF16).astype(F32))
            q_inv[j, pl.ds(row, 1), :] = query_scale
            project_keys(raw[CH:], row + 2, 2, j, ks, vs, k_inv)
            put(ogs, j, row + 2, out_both[:, j * PIX : (j + 1) * PIX])

    each_row(ROWS, (visit,))


def forward_kernel(
    side, left, right, row_halo, left_corner, right_corner, gain, w_in, ogs, qs,
    ks_in, vs_in, k_inv_in, normed_in,
    ks, vs, k_inv, normed, weights, prob_grads, attended, stats,
):
    halo_row, _, _ = halo_start(side)
    gain_full = gain[...]
    w_keys = w_in[CH:, :]

    def piece(ref, offset, first, col):
        def one(row):
            views = normed_views(ref, row, gain_full)
            both = jnp.dot(w_keys, jnp.concatenate(views, axis=1), preferred_element_type=F32)
            for j in range(2):
                normed[row + first, col + j] = views[j]
                project_keys(both[:, j * PIX : (j + 1) * PIX], row + offset, col, j, ks, vs, k_inv)

        return one

    each_row(ROWS, (piece(left, 2, 0, 0), piece(right, 2, 0, 4)))
    each_row(
        2,
        (
            piece(row_halo, halo_row, ROWS, 2),
            piece(left_corner, halo_row, ROWS, 0),
            piece(right_corner, halo_row, ROWS, 4),
        ),
    )

    def attend(step, carry):
        col, head = step // HEADS, step % HEADS
        base = head * (SIZE * S)
        query = [take(qs, col, base + d * S + 2) * SCALE for d in range(SIZE)]
        og = [take(ogs, col, base + d * S + 2) for d in range(SIZE)]
        acc = [jnp.zeros((ROWS, PIX), F32)] * SIZE
        exp_total = jnp.zeros((ROWS, PIX), F32)
        spread = jnp.zeros((ROWS, PIX), F32)
        for j in range(5):
            for i in range(5):
                key = [take(ks, col + j, base + d * S + i) for d in range(SIZE)]
                weight = jnp.exp(total(a * b for a, b in zip(query, key)))
                value = [take(vs, col + j, base + d * S + i) for d in range(SIZE)]
                prob_grad = total(a * b for a, b in zip(og, value))
                acc = [a + weight * b for a, b in zip(acc, value)]
                exp_total = exp_total + weight
                spread = spread + weight * prob_grad
                weights[step, 5 * j + i] = weight
                prob_grads[step, 5 * j + i] = prob_grad
        inv_total = 1.0 / exp_total
        for d in range(SIZE):
            attended[col, pl.ds((head * SIZE + d) * R, ROWS), :] = acc[d] * inv_total
        stats[0, step] = inv_total
        stats[1, step] = spread * inv_total
        return carry

    lax.fori_loop(0, COLS * HEADS, attend, 0)


def unit_back(unit, scale, upstream):
    mean = jnp.sum(upstream * unit, axis=0, keepdims=True) * (1.0 / CH)
    return scale[None] * (upstream - unit * mean)


def window(ref, col, row):
    return jnp.stack([take(ref, col, d * S + row) for d in range(CH)], axis=0)


def outer(left, right):
    return lax.dot_general(left, right, (((1,), (1,)), ((), ())), preferred_element_type=F32)


def view(ref, col, row, channels):
    return ref[col, pl.ds(row, channels, stride=R), :].astype(BF16)


def gradient_kernel(
    side, qs, ks, ogs, q_inv, k_inv, normed, weights, prob_grads, attended, stats, cot,
    weight_sums, raw_query, to_left, to_right, own_raw,
    probs, score_grads, grads, raws, halo_grads, halo_raws,
):
    _, _, edge_row = halo_start(side)
    zeros = jnp.zeros((ROWS, PIX), F32)
    pads = jnp.zeros((25, PIX), F32)

    def query_one(step, carry):
        col, head = step // HEADS, step % HEADS
        base = head * (SIZE * S)
        for ref in (probs, score_grads):
            for row in (0, 1, 10, 11):
                ref[step, pl.ds(row, 25, stride=W), :] = pads
        inv_total, spread = stats[0, step], stats[1, step]
        acc = [zeros] * SIZE
        for j in range(5):
            for i in range(5):
                o = 5 * j + i
                prob = weights[step, o] * inv_total
                score_grad = prob * (prob_grads[step, o] - spread)
                probs[step, pl.ds(o * W + 2, ROWS), :] = prob
                score_grads[step, pl.ds(o * W + 2, ROWS), :] = score_grad
                acc = [a + score_grad * take(ks, col + j, base + d * S + i) for d, a in enumerate(acc)]
        for d in range(SIZE):
            grads[col, head * SIZE + d] = acc[d]
        return carry

    lax.fori_loop(0, COLS * HEADS, query_one, 0)

    def query_finish(col, carry):
        raw = unit_back(window(qs, col, 2), q_inv[col] * SCALE, grads[col])
        for d in range(CH):
            raws[col, pl.ds(d * R, ROWS), :] = raw[d]
        return carry

    lax.fori_loop(0, COLS, query_finish, 0)

    def query_sums(half, carry):
        query_acc, out_acc = carry
        raw, mixed, normed_all, cot_all = [], [], [], []
        for row in (2 * half, 2 * half + 1):
            for j in range(2):
                raw.append(view(raws, j, row, CH))
                raw_query[row, j] = raw[-1]
                mixed.append(view(attended, j, row, CH))
                normed_all.append(normed[row, 2 + j])
                cot_all.append(cot[row, j])
        raw, mixed, normed_all, cot_all = (
            jnp.concatenate(x, axis=1) for x in (raw, mixed, normed_all, cot_all)
        )
        return query_acc + outer(normed_all, raw), out_acc + outer(mixed, cot_all)

    flat = jnp.zeros((CH, CH), F32)
    query_acc, out_acc = lax.fori_loop(0, ROWS // 2, query_sums, (flat, flat))
    weight_sums[CH : 2 * CH, :] = jnp.concatenate([query_acc, out_acc], axis=1)

    def key_step(acc, step, col, j, i, base, first_row):
        key_acc, value_acc = acc
        start = first_row - i + 2
        prob = probs[step, pl.ds((5 * j + i) * W + start, ROWS), :]
        score_grad = score_grads[step, pl.ds((5 * j + i) * W + start, ROWS), :]
        key_acc = [a + score_grad * take(qs, col, base + d * S + start) for d, a in enumerate(key_acc)]
        value_acc = [a + prob * take(ogs, col, base + d * S + start) for d, a in enumerate(value_acc)]
        return key_acc, value_acc

    edge_first, edge_offset = edge_row * 2 // 3, edge_row // 2

    def key_columns(view_col, head, cols):
        base = head * (SIZE * S)
        own_steps = [(i, 2) for i in range(5)]
        halo_steps = [(edge_offset + i, edge_first) for i in range(2)]
        for steps, key_ref, value_ref in (
            (own_steps, grads, raws), (halo_steps, halo_grads, halo_raws)
        ):
            acc = ([zeros] * SIZE, [zeros] * SIZE)
            for col in cols:
                for i, first_row in steps:
                    acc = key_step(acc, col * HEADS + head, col, view_col - col, i, base, first_row)
            for d in range(SIZE):
                key_ref[view_col, head * SIZE + d] = acc[0][d]
                value_ref[view_col, pl.ds((CH + head * SIZE + d) * R, ROWS), :] = acc[1][d]

    def inner_columns(step, carry):
        key_columns(1 + step // HEADS, step % HEADS, (0, 1))
        return carry

    def outer_columns(step, carry):
        side_col = step // HEADS
        key_columns(5 * side_col, step % HEADS, (side_col,))
        return carry

    lax.fori_loop(0, 4 * HEADS, inner_columns, 0)
    lax.fori_loop(0, 2 * HEADS, outer_columns, 0)

    def key_finish(col, carry):
        for source, target, row in ((grads, raws, 2), (halo_grads, halo_raws, edge_first)):
            scale = k_inv[col, pl.ds(row, ROWS), :] * SCALE
            raw = unit_back(window(ks, col, row), scale, source[col])
            for d in range(CH):
                target[col, pl.ds(d * R, ROWS), :] = raw[d]
        return carry

    lax.fori_loop(0, 6, key_finish, 0)

    def key_sums(source, from_row, first):
        def one(row, acc):
            raw = [view(source, col, row + from_row, 2 * CH) for col in range(6)]
            for col in range(6):
                (to_left, own_raw, to_right)[col // 2][row + first, col % 2] = raw[col]
            normed_all = [normed[row + first, col] for col in range(6)]
            return acc + outer(jnp.concatenate(normed_all, axis=1), jnp.concatenate(raw, axis=1))

        return one

    acc = lax.fori_loop(0, ROWS, key_sums(raws, 0, 0), jnp.zeros((CH, 2 * CH), F32))
    weight_sums[0:CH, :] = lax.fori_loop(0, 2, key_sums(halo_raws, edge_row, ROWS), acc)


def row_kernel(own_raw, left_raw, right_raw, row_send):
    for row in range(2):
        for j in range(2):
            row_send[row, j] = sum(
                x[ROWS + row, j].astype(F32) for x in (own_raw, left_raw, right_raw)
            ).astype(BF16)


def features_kernel(
    side, own_raw, left_raw, right_raw, row_raw, raw_query, feats, cot, gain, w_back,
    feats_grad, shared,
):
    _, _, edge_row = halo_start(side)

    def join(row):
        for j in range(2):
            shared[row, j] = (
                own_raw[row, j].astype(F32) + left_raw[row, j].astype(F32)
                + right_raw[row, j].astype(F32)
            )

    def join_edge(row):
        for j in range(2):
            shared[row + edge_row, j] = shared[row + edge_row, j] + row_raw[row, j].astype(F32)

    each_row(ROWS, (join,))
    each_row(2, (join_edge,))
    gain_full = gain[...]
    w_b = w_back[...]

    def view_row(row):
        raw = jnp.concatenate([pair(raw_query, row), pair(shared, row).astype(BF16)], axis=0)
        normed_grad = jnp.dot(w_b, raw, preferred_element_type=F32)
        for j in range(2):
            values = feats[row, j].astype(F32)
            inv_norm = inv_rms(values)
            scaled = values * inv_norm
            scaled_grad = normed_grad[:, j * PIX : (j + 1) * PIX] * gain_full
            mean = jnp.mean(scaled_grad * scaled, axis=0, keepdims=True)
            branch = inv_norm * (scaled_grad - scaled * mean)
            feats_grad[row, j] = (cot[row, j].astype(F32) + branch).astype(BF16)

    each_row(ROWS, (view_row,))


def last_kernel(factor, sums, w_q, w_kv, gain, query_grad, keyval_grad, output_grad, gain_grad):
    keyval = sums[0:CH, :] * factor
    rest = sums[CH : 2 * CH, :] * factor
    query = rest[:, :CH]
    keyval_grad[...] = keyval
    query_grad[...] = query
    output_grad[...] = rest[:, CH:]
    col = jnp.sum(query * w_q[...].astype(F32), axis=1, keepdims=True) + jnp.sum(
        keyval * w_kv[...].astype(F32), axis=1, keepdims=True
    )
    line = jnp.sum(jnp.where(eye(), jnp.broadcast_to(col, (CH, CH)), 0.0), axis=0, keepdims=True)
    gain_grad[...] = line / gain[...]


def call(kernel, outs, scratch, flops, *operands, aliases=(), far=()):
    return pl.pallas_call(
        kernel,
        out_shape=[jax.ShapeDtypeStruct(shape, dtype) for shape, dtype in outs],
        in_specs=[
            SM if x.dtype == jnp.int32 else FAR if k in far else VM for k, x in enumerate(operands)
        ],
        out_specs=[VM] * len(outs),
        scratch_shapes=[pltpu.VMEM(x, F32) if isinstance(x, tuple) else x for x in scratch],
        input_output_aliases=dict(aliases),
        compiler_params=pltpu.CompilerParams(vmem_limit_bytes=20 * 1024 * 1024),
        cost_estimate=pl.CostEstimate(flops=flops, bytes_accessed=1000000, transcendentals=0),
    )(*operands)


def near_memory(x):
    return pltpu.with_memory_space_constraint(x, pltpu.VMEM)


def sum_kernel(shares, copies):
    share = jnp.sum(shares[...].astype(F32), axis=0).astype(copies.dtype)
    for k in range(copies.shape[0]):
        copies[k] = share


def sum_everywhere(values):
    near, far = ("px", "pc", "vrow"), ("py", "vcol")
    near_count, far_count = (math.prod(lax.axis_size(a) for a in axes) for axes in (near, far))
    size = values.size // (near_count * PIX)

    def exchange(copies, axes):
        return near_memory(lax.all_to_all(copies, axes, 0, 0))

    shares = exchange(values.reshape(near_count, size, PIX), near)
    (copies,) = call(sum_kernel, [((far_count, size, PIX), BF16)], [], 100000, shares)
    shares = exchange(copies, far)
    (copies,) = call(sum_kernel, [((near_count, size, PIX), F32)], [], 100000, shares)
    return lax.all_to_all(copies, near, 0, 0).reshape(values.shape)


def layer(features, out_cotangent, norm_gain, query_proj, keyval_proj, output_proj):
    side = lax.axis_index("vrow").astype(jnp.int32).reshape(1)
    cols = lax.axis_size("vcol")
    up = [(i, i + 1) for i in range(cols - 1)]
    down = [(j, i) for i, j in up]
    cross = [(0, 1), (1, 0)]
    diag_up = [(a * cols + i, b * cols + j) for a, b in cross for i, j in up]
    diag_down = [(a * cols + i, b * cols + j) for a, b in cross for i, j in down]
    grid = ("vrow", "vcol")
    gain = norm_gain.reshape(1, CH)
    held = [
        pltpu.with_memory_space_constraint(x, pltpu.HBM)
        for x in (features, out_cotangent, gain, query_proj, keyval_proj, output_proj)
    ]

    left = lax.ppermute(features, "vcol", up)
    right = lax.ppermute(features, "vcol", down)
    (edge,) = call(
        edge_kernel, [((2, COLS, CH, PIX), BF16)], [pltpu.SemaphoreType.DMA], 1000, side, held[0],
        far=(1,),
    )
    row_halo = lax.ppermute(edge, "vrow", cross)
    left_corner = lax.ppermute(edge, grid, diag_up)
    right_corner = lax.ppermute(edge, grid, diag_down)

    own = ((COLS, CH * S, PIX), F32)
    padded = ((6, CH * S, PIX), F32)
    lanes = ((COLS, ROWS, PIX), F32)
    key_lanes = ((6, 16, PIX), F32)
    steps = COLS * HEADS
    offsets = ((steps, 25, ROWS, PIX), F32)
    views = ((ROWS, COLS, CH, PIX), BF16)
    all_views = ((ROWS + 2, 6, CH, PIX), BF16)
    key_views = ((ROWS + 2, COLS, 2 * CH, PIX), BF16)
    (
        qs, ks, vs, ogs, q_inv, k_inv, normed, gain_full, w_in, w_back, feats, cot, w_q, w_kv, gain_row,
    ) = call(
        own_kernel,
        [
            own, padded, padded, own, lanes, key_lanes, all_views, ((CH, PIX), F32),
            ((3 * CH, CH), BF16), ((CH, 3 * CH), BF16), views, views, ((CH, CH), BF16),
            ((CH, 2 * CH), BF16), ((1, CH), F32),
        ],
        [pltpu.VMEM((CH, CH), BF16), pltpu.SemaphoreType.DMA((6,))], 2000000,
        side, *held, far=(1, 2, 3, 4, 5, 6),
    )
    ks, vs, k_inv, normed, weights, prob_grads, attended, stats = call(
        forward_kernel,
        [
            padded, padded, key_lanes, all_views, offsets, offsets,
            ((COLS, CH * R, PIX), F32), ((2, steps, ROWS, PIX), F32),
        ],
        [], 4000000,
        side, left, right, row_halo, left_corner, right_corner, gain_full, w_in, ogs, qs,
        ks, vs, k_inv, normed,
        aliases=((10, 0), (11, 1), (12, 2), (13, 3)),
    )
    weight_sums, raw_query, to_left, to_right, own_raw = call(
        gradient_kernel,
        [((2 * CH, PIX), F32), views, key_views, key_views, key_views],
        [
            (steps, 25 * W, PIX), (steps, 25 * W, PIX), (6, CH, ROWS, PIX), (6, 2 * CH * R, PIX),
            (6, CH, ROWS, PIX), (6, 2 * CH * R, PIX),
        ],
        5000000,
        side, qs, ks, ogs, q_inv, k_inv, normed, weights, prob_grads, attended, stats, cot,
    )
    sums = sum_everywhere(weight_sums)
    right_raw = lax.ppermute(pltpu.with_memory_space_constraint(to_left, pltpu.HBM), "vcol", down)
    left_raw = lax.ppermute(pltpu.with_memory_space_constraint(to_right, pltpu.HBM), "vcol", up)
    (row_send,) = call(
        row_kernel, [((2, COLS, 2 * CH, PIX), BF16)], [], 10000, own_raw, left_raw, right_raw
    )
    row_raw = lax.ppermute(row_send, "vrow", cross)
    (features_grad,) = call(
        features_kernel, [(features.shape, BF16)], [(ROWS, COLS, 2 * CH, PIX)], 2000000,
        side, own_raw, left_raw, right_raw, row_raw, raw_query, feats, cot, gain_full, w_back,
    )
    tokens_all = ROWS * COLS * PIX * math.prod(lax.axis_size(a) for a in AXES)
    query_grad, keyval_grad, output_grad, gain_grad = call(
        functools.partial(last_kernel, 1.0 / math.sqrt(tokens_all)),
        [((CH, CH), F32), ((CH, 2 * CH), F32), ((CH, CH), F32), ((1, CH), F32)],
        [], 100000,
        sums, w_q, w_kv, gain_row,
    )
    return features_grad, query_grad, keyval_grad, output_grad, gain_grad.reshape(CH)


def solution(mesh):
    rows, cols, _ = mesh.devices.shape
    parts = jax.sharding.Mesh(mesh.devices.reshape(rows, cols, 4, 4, 2), AXES)
    placed = P("vrow", "vcol", None, AXES[2:])
    return jax.shard_map(
        layer,
        mesh=parts,
        in_specs=(placed, placed, P(), P(), P(), P()),
        out_specs=(placed, P(), P(), P(), P()),
        check_vma=False,
    )
```

```python
import functools
import math

import jax
import jax.numpy as jnp
from jax import lax
from jax.experimental import pallas as pl
from jax.experimental.pallas import tpu as pltpu
from jax.sharding import PartitionSpec as P


AXES = ("vrow", "vcol", "px", "py", "pc")
HEADS = 4
SIZE = 16
CH = 64
ROWS = 8
COLS = 2
PIX = 128
S = 13
W = 13
R = 9
EPSILON = 1e-06
SCALE = SIZE ** (-0.5)
F32 = jnp.float32
BF16 = jnp.bfloat16

VM = pl.BlockSpec(memory_space=pltpu.VMEM)
FAR = pl.BlockSpec(memory_space=pltpu.HBM)
SM = pl.BlockSpec(memory_space=pltpu.SMEM)


def inv_rms(values):
    return lax.rsqrt(jnp.mean(values * values, axis=0, keepdims=True) + EPSILON)


def total(terms):
    terms = list(terms)
    while len(terms) > 1:
        terms = [a + b for a, b in zip(terms[::2], terms[1::2])] + (
            [terms[-1]] if len(terms) % 2 else []
        )
    return terms[0]


def put(ref, col, row, values):
    ref[col, pl.ds(row, values.shape[0], stride=S), :] = values


def take(ref, col, start):
    return ref[col, pl.ds(start, ROWS), :]


def pair(ref, row, first=0):
    return jnp.concatenate([ref[row, first], ref[row, first + 1]], axis=1)


def each_row(count, visits):
    def one(row, carry):
        for visit in visits:
            visit(row)
        return carry

    lax.fori_loop(0, count, one, 0)


def halo_start(side_ref):
    side = jnp.right_shift(side_ref[0], 1)
    return 10 - 10 * side, 10 * side, 6 - 6 * side


def partner_cols(side_ref):
    odd = jnp.bitwise_and(side_ref[0], 1)
    return 4 - 4 * odd, 4 * odd


def clear_rows(refs, row):
    for ref in refs:
        zeros = jnp.zeros((ref.shape[1] // S, PIX), F32)
        for col in range(ref.shape[0]):
            put(ref, col, row, zeros)
            put(ref, col, row + 1, zeros)


def eye():
    shape = (CH, CH)
    return lax.broadcasted_iota(jnp.int32, shape, 0) == lax.broadcasted_iota(jnp.int32, shape, 1)


def normed_views(ref, row, gain):
    out = []
    for j in range(2):
        values = ref[row, j].astype(F32)
        out.append((values * inv_rms(values) * gain).astype(BF16))
    return out


def project_keys(raw, to_row, col, j, ks, vs, k_inv):
    key, value = raw[:CH], raw[CH:]
    key_scale = inv_rms(key)
    put(ks, col + j, to_row, (key * key_scale).astype(BF16).astype(F32))
    put(vs, col + j, to_row, value.astype(BF16).astype(F32))
    k_inv[col + j, pl.ds(to_row, 1), :] = key_scale


def edge_kernel(side, feats, edge, sem):
    _, _, edge_row = halo_start(side)
    copy = pltpu.make_async_copy(feats.at[pl.ds(edge_row, 2)], edge, sem)
    copy.start()
    copy.wait()


def own_kernel(
    side, feats_hbm, cot_hbm, gain_hbm, w_q_hbm, w_kv_hbm, w_out_hbm,
    qs, ks, vs, ogs, q_inv, k_inv, normed, gain_out, w_in, w_back, feats, cot, w_q, w_kv, gain_row,
    w_out, sems,
):
    moves = (
        (gain_hbm, gain_row), (w_q_hbm, w_q), (w_kv_hbm, w_kv), (w_out_hbm, w_out),
        (feats_hbm, feats), (cot_hbm, cot),
    )
    copies = [pltpu.make_async_copy(a, b, sems.at[k]) for k, (a, b) in enumerate(moves)]
    for copy in copies:
        copy.start()
    _, clear_row, _ = halo_start(side)
    clear_rows((ks, vs), clear_row)
    clear_rows((qs, ogs), 0)
    clear_rows((qs, ogs), 10)
    for copy in copies[:4]:
        copy.wait()
    gain_col = jnp.sum(
        jnp.where(eye(), jnp.broadcast_to(gain_row[...], (CH, CH)), 0.0), axis=1, keepdims=True
    )
    gain_full = jnp.broadcast_to(gain_col, (CH, PIX))
    gain_out[...] = gain_full
    w_in[0:CH, :] = w_q[...].astype(F32).T.astype(BF16)
    w_in[CH:, :] = w_kv[...].astype(F32).T.astype(BF16)
    w_back[...] = jnp.concatenate([w_q[...].astype(F32), w_kv[...].astype(F32)], axis=1).astype(BF16)
    w_full = w_in[...]
    w_o = w_out[...]
    for copy in copies[4:]:
        copy.wait()

    def visit(row):
        views = normed_views(feats, row, gain_full)
        both = jnp.dot(w_full, jnp.concatenate(views, axis=1), preferred_element_type=F32)
        out_both = jnp.dot(w_o, pair(cot, row), preferred_element_type=F32)
        for j in range(2):
            normed[row, 2 + j] = views[j]
            raw = both[:, j * PIX : (j + 1) * PIX]
            query_scale = inv_rms(raw[:CH])
            put(qs, j, row + 2, (raw[:CH] * query_scale).astype(BF16).astype(F32))
            q_inv[j, pl.ds(row, 1), :] = query_scale
            project_keys(raw[CH:], row + 2, 2, j, ks, vs, k_inv)
            put(ogs, j, row + 2, out_both[:, j * PIX : (j + 1) * PIX])

    each_row(ROWS, (visit,))


def forward_kernel(
    side, first, second, row_halo, first_corner, second_corner, gain, w_in, ogs, qs,
    ks_in, vs_in, k_inv_in, normed_in,
    ks, vs, k_inv, normed, weights, prob_grads, attended, stats,
):
    halo_row, _, _ = halo_start(side)
    first_col, second_col = partner_cols(side)
    gain_full = gain[...]
    w_keys = w_in[CH:, :]

    def piece(ref, offset, to_row, col):
        def one(row):
            views = normed_views(ref, row, gain_full)
            both = jnp.dot(w_keys, jnp.concatenate(views, axis=1), preferred_element_type=F32)
            for j in range(2):
                normed[row + to_row, col + j] = views[j]
                project_keys(both[:, j * PIX : (j + 1) * PIX], row + offset, col, j, ks, vs, k_inv)

        return one

    each_row(ROWS, (piece(first, 2, 0, first_col), piece(second, 2, 0, second_col)))
    each_row(
        2,
        (
            piece(row_halo, halo_row, ROWS, 2),
            piece(first_corner, halo_row, ROWS, first_col),
            piece(second_corner, halo_row, ROWS, second_col),
        ),
    )

    def attend(step, carry):
        col, head = step // HEADS, step % HEADS
        base = head * (SIZE * S)
        query = [take(qs, col, base + d * S + 2) * SCALE for d in range(SIZE)]
        og = [take(ogs, col, base + d * S + 2) for d in range(SIZE)]
        acc = [jnp.zeros((ROWS, PIX), F32)] * SIZE
        exp_total = jnp.zeros((ROWS, PIX), F32)
        spread = jnp.zeros((ROWS, PIX), F32)
        for j in range(5):
            for i in range(5):
                key = [take(ks, col + j, base + d * S + i) for d in range(SIZE)]
                weight = jnp.exp(total(a * b for a, b in zip(query, key)))
                value = [take(vs, col + j, base + d * S + i) for d in range(SIZE)]
                prob_grad = total(a * b for a, b in zip(og, value))
                acc = [a + weight * b for a, b in zip(acc, value)]
                exp_total = exp_total + weight
                spread = spread + weight * prob_grad
                weights[step, 5 * j + i] = weight
                prob_grads[step, 5 * j + i] = prob_grad
        inv_total = 1.0 / exp_total
        for d in range(SIZE):
            attended[col, pl.ds((head * SIZE + d) * R, ROWS), :] = acc[d] * inv_total
        stats[0, step] = inv_total
        stats[1, step] = spread * inv_total
        return carry

    lax.fori_loop(0, COLS * HEADS, attend, 0)


def unit_back(unit, scale, upstream):
    mean = jnp.sum(upstream * unit, axis=0, keepdims=True) * (1.0 / CH)
    return scale[None] * (upstream - unit * mean)


def window(ref, col, row):
    return jnp.stack([take(ref, col, d * S + row) for d in range(CH)], axis=0)


def outer(left, right):
    return lax.dot_general(left, right, (((1,), (1,)), ((), ())), preferred_element_type=F32)


def view(ref, col, row, channels):
    return ref[col, pl.ds(row, channels, stride=R), :].astype(BF16)


def gradient_kernel(
    side, qs, ks, ogs, q_inv, k_inv, normed, weights, prob_grads, attended, stats, cot,
    weight_sums, raw_query, to_first, to_second, own_raw,
    probs, score_grads, grads, raws, halo_grads, halo_raws,
):
    _, _, edge_row = halo_start(side)
    first_col, second_col = partner_cols(side)
    zeros = jnp.zeros((ROWS, PIX), F32)
    pads = jnp.zeros((25, PIX), F32)

    def query_one(step, carry):
        col, head = step // HEADS, step % HEADS
        base = head * (SIZE * S)
        for ref in (probs, score_grads):
            for row in (0, 1, 10, 11):
                ref[step, pl.ds(row, 25, stride=W), :] = pads
        inv_total, spread = stats[0, step], stats[1, step]
        acc = [zeros] * SIZE
        for j in range(5):
            for i in range(5):
                o = 5 * j + i
                prob = weights[step, o] * inv_total
                score_grad = prob * (prob_grads[step, o] - spread)
                probs[step, pl.ds(o * W + 2, ROWS), :] = prob
                score_grads[step, pl.ds(o * W + 2, ROWS), :] = score_grad
                acc = [a + score_grad * take(ks, col + j, base + d * S + i) for d, a in enumerate(acc)]
        for d in range(SIZE):
            grads[col, head * SIZE + d] = acc[d]
        return carry

    lax.fori_loop(0, COLS * HEADS, query_one, 0)

    def query_finish(col, carry):
        raw = unit_back(window(qs, col, 2), q_inv[col] * SCALE, grads[col])
        for d in range(CH):
            raws[col, pl.ds(d * R, ROWS), :] = raw[d]
        return carry

    lax.fori_loop(0, COLS, query_finish, 0)

    def query_sums(half, carry):
        query_acc, out_acc = carry
        raw, mixed, normed_all, cot_all = [], [], [], []
        for row in (2 * half, 2 * half + 1):
            for j in range(2):
                raw.append(view(raws, j, row, CH))
                raw_query[row, j] = raw[-1]
                mixed.append(view(attended, j, row, CH))
                normed_all.append(normed[row, 2 + j])
                cot_all.append(cot[row, j])
        raw, mixed, normed_all, cot_all = (
            jnp.concatenate(x, axis=1) for x in (raw, mixed, normed_all, cot_all)
        )
        return query_acc + outer(normed_all, raw), out_acc + outer(mixed, cot_all)

    flat = jnp.zeros((CH, CH), F32)
    query_acc, out_acc = lax.fori_loop(0, ROWS // 2, query_sums, (flat, flat))
    weight_sums[CH : 2 * CH, :] = jnp.concatenate([query_acc, out_acc], axis=1)

    def key_step(acc, step, col, j, i, base, first_row):
        key_acc, value_acc = acc
        start = first_row - i + 2
        prob = probs[step, pl.ds((5 * j + i) * W + start, ROWS), :]
        score_grad = score_grads[step, pl.ds((5 * j + i) * W + start, ROWS), :]
        key_acc = [a + score_grad * take(qs, col, base + d * S + start) for d, a in enumerate(key_acc)]
        value_acc = [a + prob * take(ogs, col, base + d * S + start) for d, a in enumerate(value_acc)]
        return key_acc, value_acc

    edge_first, edge_offset = edge_row * 2 // 3, edge_row // 2

    def key_columns(view_col, head, cols):
        base = head * (SIZE * S)
        own_steps = [(i, 2) for i in range(5)]
        halo_steps = [(edge_offset + i, edge_first) for i in range(2)]
        for steps, key_ref, value_ref in (
            (own_steps, grads, raws), (halo_steps, halo_grads, halo_raws)
        ):
            acc = ([zeros] * SIZE, [zeros] * SIZE)
            for col in cols:
                for i, first_row in steps:
                    acc = key_step(acc, col * HEADS + head, col, view_col - col, i, base, first_row)
            for d in range(SIZE):
                key_ref[view_col, head * SIZE + d] = acc[0][d]
                value_ref[view_col, pl.ds((CH + head * SIZE + d) * R, ROWS), :] = acc[1][d]

    def inner_columns(step, carry):
        key_columns(1 + step // HEADS, step % HEADS, (0, 1))
        return carry

    def outer_columns(step, carry):
        side_col = step // HEADS
        key_columns(5 * side_col, step % HEADS, (side_col,))
        return carry

    lax.fori_loop(0, 4 * HEADS, inner_columns, 0)
    lax.fori_loop(0, 2 * HEADS, outer_columns, 0)

    def key_finish(col, carry):
        for source, target, row in ((grads, raws, 2), (halo_grads, halo_raws, edge_first)):
            scale = k_inv[col, pl.ds(row, ROWS), :] * SCALE
            raw = unit_back(window(ks, col, row), scale, source[col])
            for d in range(CH):
                target[col, pl.ds(d * R, ROWS), :] = raw[d]
        return carry

    lax.fori_loop(0, 6, key_finish, 0)

    def key_sums(source, from_row, first):
        def one(row, acc):
            raw, normed_all = [], []
            for target, col in ((to_first, first_col), (own_raw, 2), (to_second, second_col)):
                for j in range(2):
                    raw.append(view(source, col + j, row + from_row, 2 * CH))
                    target[row + first, j] = raw[-1]
                    normed_all.append(normed[row + first, col + j])
            return acc + outer(jnp.concatenate(normed_all, axis=1), jnp.concatenate(raw, axis=1))

        return one

    acc = lax.fori_loop(0, ROWS, key_sums(raws, 0, 0), jnp.zeros((CH, 2 * CH), F32))
    weight_sums[0:CH, :] = lax.fori_loop(0, 2, key_sums(halo_raws, edge_row, ROWS), acc)


def row_kernel(own_raw, first_raw, second_raw, row_send):
    for row in range(2):
        for j in range(2):
            row_send[row, j] = sum(
                x[ROWS + row, j].astype(F32) for x in (own_raw, first_raw, second_raw)
            ).astype(BF16)


def features_kernel(
    side, own_raw, first_raw, second_raw, row_raw, raw_query, feats, cot, gain, w_back,
    feats_grad, shared,
):
    _, _, edge_row = halo_start(side)

    def join(row):
        for j in range(2):
            shared[row, j] = (
                own_raw[row, j].astype(F32) + first_raw[row, j].astype(F32)
                + second_raw[row, j].astype(F32)
            )

    def join_edge(row):
        for j in range(2):
            shared[row + edge_row, j] = shared[row + edge_row, j] + row_raw[row, j].astype(F32)

    each_row(ROWS, (join,))
    each_row(2, (join_edge,))
    gain_full = gain[...]
    w_b = w_back[...]

    def view_row(row):
        raw = jnp.concatenate([pair(raw_query, row), pair(shared, row).astype(BF16)], axis=0)
        normed_grad = jnp.dot(w_b, raw, preferred_element_type=F32)
        for j in range(2):
            values = feats[row, j].astype(F32)
            inv_norm = inv_rms(values)
            scaled = values * inv_norm
            scaled_grad = normed_grad[:, j * PIX : (j + 1) * PIX] * gain_full
            mean = jnp.mean(scaled_grad * scaled, axis=0, keepdims=True)
            branch = inv_norm * (scaled_grad - scaled * mean)
            feats_grad[row, j] = (cot[row, j].astype(F32) + branch).astype(BF16)

    each_row(ROWS, (view_row,))


def last_kernel(factor, sums, w_q, w_kv, gain, query_grad, keyval_grad, output_grad, gain_grad):
    keyval = sums[0:CH, :] * factor
    rest = sums[CH : 2 * CH, :] * factor
    query = rest[:, :CH]
    keyval_grad[...] = keyval
    query_grad[...] = query
    output_grad[...] = rest[:, CH:]
    col = jnp.sum(query * w_q[...].astype(F32), axis=1, keepdims=True) + jnp.sum(
        keyval * w_kv[...].astype(F32), axis=1, keepdims=True
    )
    line = jnp.sum(jnp.where(eye(), jnp.broadcast_to(col, (CH, CH)), 0.0), axis=0, keepdims=True)
    gain_grad[...] = line / gain[...]


def call(kernel, outs, scratch, flops, *operands, aliases=(), far=()):
    return pl.pallas_call(
        kernel,
        out_shape=[jax.ShapeDtypeStruct(shape, dtype) for shape, dtype in outs],
        in_specs=[
            SM if x.dtype == jnp.int32 else FAR if k in far else VM for k, x in enumerate(operands)
        ],
        out_specs=[VM] * len(outs),
        scratch_shapes=[pltpu.VMEM(x, F32) if isinstance(x, tuple) else x for x in scratch],
        input_output_aliases=dict(aliases),
        compiler_params=pltpu.CompilerParams(vmem_limit_bytes=20 * 1024 * 1024),
        cost_estimate=pl.CostEstimate(flops=flops, bytes_accessed=1000000, transcendentals=0),
    )(*operands)


def near_memory(x):
    return pltpu.with_memory_space_constraint(x, pltpu.VMEM)


def sum_kernel(shares, copies):
    share = jnp.sum(shares[...].astype(F32), axis=0).astype(copies.dtype)
    for k in range(copies.shape[0]):
        copies[k] = share


def sum_everywhere(values):
    near, far = ("px", "pc", "vrow"), ("py", "vcol")
    near_count, far_count = (math.prod(lax.axis_size(a) for a in axes) for axes in (near, far))
    size = values.size // (near_count * PIX)

    def exchange(copies, axes):
        return near_memory(lax.all_to_all(copies, axes, 0, 0))

    shares = exchange(values.reshape(near_count, size, PIX), near)
    (copies,) = call(sum_kernel, [((far_count, size, PIX), BF16)], [], 100000, shares)
    shares = exchange(copies, far)
    (copies,) = call(sum_kernel, [((near_count, size, PIX), F32)], [], 100000, shares)
    return lax.all_to_all(copies, near, 0, 0).reshape(values.shape)


def layer(features, out_cotangent, norm_gain, query_proj, keyval_proj, output_proj):
    place = lax.axis_index("vrow") * 2 + jnp.bitwise_and(lax.axis_index("vcol"), 1)
    side = place.astype(jnp.int32).reshape(1)
    cols = lax.axis_size("vcol")
    grid = ("vrow", "vcol")

    def both_ways(pairs):
        return [*pairs, *((b, a) for a, b in pairs)]

    rounds = [[(i, i + 1) for i in range(start, cols - 1, 2)] for start in (0, 1)]
    first_swap, second_swap = (both_ways(pairs) for pairs in rounds)
    first_cross, second_cross = (
        [(a * cols + i, (1 - a) * cols + j) for a in (0, 1) for i, j in swap]
        for swap in (first_swap, second_swap)
    )
    row_swap = both_ways([(0, 1)])
    gain = norm_gain.reshape(1, CH)
    held = [
        pltpu.with_memory_space_constraint(x, pltpu.HBM)
        for x in (features, out_cotangent, gain, query_proj, keyval_proj, output_proj)
    ]

    first = lax.ppermute(features, "vcol", first_swap)
    second = lax.ppermute(features, "vcol", second_swap)
    (edge,) = call(
        edge_kernel, [((2, COLS, CH, PIX), BF16)], [pltpu.SemaphoreType.DMA], 1000, side, held[0],
        far=(1,),
    )
    row_halo = lax.ppermute(edge, "vrow", row_swap)
    first_corner = lax.ppermute(edge, grid, first_cross)
    second_corner = lax.ppermute(edge, grid, second_cross)

    own = ((COLS, CH * S, PIX), F32)
    padded = ((6, CH * S, PIX), F32)
    lanes = ((COLS, ROWS, PIX), F32)
    key_lanes = ((6, 16, PIX), F32)
    steps = COLS * HEADS
    offsets = ((steps, 25, ROWS, PIX), F32)
    views = ((ROWS, COLS, CH, PIX), BF16)
    all_views = ((ROWS + 2, 6, CH, PIX), BF16)
    key_views = ((ROWS + 2, COLS, 2 * CH, PIX), BF16)
    (
        qs, ks, vs, ogs, q_inv, k_inv, normed, gain_full, w_in, w_back, feats, cot, w_q, w_kv, gain_row,
    ) = call(
        own_kernel,
        [
            own, padded, padded, own, lanes, key_lanes, all_views, ((CH, PIX), F32),
            ((3 * CH, CH), BF16), ((CH, 3 * CH), BF16), views, views, ((CH, CH), BF16),
            ((CH, 2 * CH), BF16), ((1, CH), F32),
        ],
        [pltpu.VMEM((CH, CH), BF16), pltpu.SemaphoreType.DMA((6,))], 2000000,
        side, *held, far=(1, 2, 3, 4, 5, 6),
    )
    ks, vs, k_inv, normed, weights, prob_grads, attended, stats = call(
        forward_kernel,
        [
            padded, padded, key_lanes, all_views, offsets, offsets,
            ((COLS, CH * R, PIX), F32), ((2, steps, ROWS, PIX), F32),
        ],
        [], 4000000,
        side, first, second, row_halo, first_corner, second_corner, gain_full, w_in, ogs, qs,
        ks, vs, k_inv, normed,
        aliases=((10, 0), (11, 1), (12, 2), (13, 3)),
    )
    weight_sums, raw_query, to_first, to_second, own_raw = call(
        gradient_kernel,
        [((2 * CH, PIX), F32), views, key_views, key_views, key_views],
        [
            (steps, 25 * W, PIX), (steps, 25 * W, PIX), (6, CH, ROWS, PIX), (6, 2 * CH * R, PIX),
            (6, CH, ROWS, PIX), (6, 2 * CH * R, PIX),
        ],
        5000000,
        side, qs, ks, ogs, q_inv, k_inv, normed, weights, prob_grads, attended, stats, cot,
    )
    sums = sum_everywhere(weight_sums)
    first_raw, second_raw = (
        lax.ppermute(pltpu.with_memory_space_constraint(x, pltpu.HBM), "vcol", swap)
        for x, swap in ((to_first, first_swap), (to_second, second_swap))
    )
    (row_send,) = call(
        row_kernel, [((2, COLS, 2 * CH, PIX), BF16)], [], 10000, own_raw, first_raw, second_raw
    )
    row_raw = lax.ppermute(row_send, "vrow", row_swap)
    (features_grad,) = call(
        features_kernel, [(features.shape, BF16)], [(ROWS, COLS, 2 * CH, PIX)], 2000000,
        side, own_raw, first_raw, second_raw, row_raw, raw_query, feats, cot, gain_full, w_back,
    )
    tokens_all = ROWS * COLS * PIX * math.prod(lax.axis_size(a) for a in AXES)
    query_grad, keyval_grad, output_grad, gain_grad = call(
        functools.partial(last_kernel, 1.0 / math.sqrt(tokens_all)),
        [((CH, CH), F32), ((CH, 2 * CH), F32), ((CH, CH), F32), ((1, CH), F32)],
        [], 100000,
        sums, w_q, w_kv, gain_row,
    )
    return features_grad, query_grad, keyval_grad, output_grad, gain_grad.reshape(CH)


def solution(mesh):
    rows, cols, _ = mesh.devices.shape
    parts = jax.sharding.Mesh(mesh.devices.reshape(rows, cols, 4, 4, 2), AXES)
    placed = P("vrow", "vcol", None, AXES[2:])
    return jax.shard_map(
        layer,
        mesh=parts,
        in_specs=(placed, placed, P(), P(), P(), P()),
        out_specs=(placed, P(), P(), P(), P()),
        check_vma=False,
    )
```

```python
import functools
import math

import jax
import jax.numpy as jnp
from jax import lax
from jax.experimental import pallas as pl
from jax.experimental.pallas import tpu as pltpu
from jax.sharding import PartitionSpec as P


AXES = ("vrow", "vcol", "px", "py", "pc")
HEADS = 4
SIZE = 16
CH = 64
ROWS = 8
COLS = 2
PIX = 128
S = 13
W = 13
R = 9
EPSILON = 1e-06
SCALE = SIZE ** (-0.5)
F32 = jnp.float32
BF16 = jnp.bfloat16

VM = pl.BlockSpec(memory_space=pltpu.VMEM)
FAR = pl.BlockSpec(memory_space=pltpu.HBM)
SM = pl.BlockSpec(memory_space=pltpu.SMEM)


def inv_rms(values):
    return lax.rsqrt(jnp.mean(values * values, axis=0, keepdims=True) + EPSILON)


def total(terms):
    terms = list(terms)
    while len(terms) > 1:
        terms = [a + b for a, b in zip(terms[::2], terms[1::2])] + (
            [terms[-1]] if len(terms) % 2 else []
        )
    return terms[0]


def put(ref, col, row, values):
    ref[col, pl.ds(row, values.shape[0], stride=S), :] = values


def take(ref, col, start):
    return ref[col, pl.ds(start, ROWS), :]


def pair(ref, row, first=0):
    return jnp.concatenate([ref[row, first], ref[row, first + 1]], axis=1)


def each_row(count, visits):
    def one(row, carry):
        for visit in visits:
            visit(row)
        return carry

    lax.fori_loop(0, count, one, 0)


def halo_start(side_ref):
    side = jnp.right_shift(side_ref[0], 1)
    return 10 - 10 * side, 10 * side, 6 - 6 * side


def partner_cols(side_ref):
    odd = jnp.bitwise_and(side_ref[0], 1)
    return 4 - 4 * odd, 4 * odd


def clear_rows(refs, row):
    for ref in refs:
        zeros = jnp.zeros((ref.shape[1] // S, PIX), F32)
        for col in range(ref.shape[0]):
            put(ref, col, row, zeros)
            put(ref, col, row + 1, zeros)


def eye():
    shape = (CH, CH)
    return lax.broadcasted_iota(jnp.int32, shape, 0) == lax.broadcasted_iota(jnp.int32, shape, 1)


def normed_views(ref, row, gain):
    out = []
    for j in range(2):
        values = ref[row, j].astype(F32)
        out.append((values * inv_rms(values) * gain).astype(BF16))
    return out


def project_keys(raw, to_row, col, j, ks, vs, k_inv):
    key, value = raw[:CH], raw[CH:]
    key_scale = inv_rms(key)
    put(ks, col + j, to_row, (key * key_scale).astype(BF16).astype(F32))
    put(vs, col + j, to_row, value.astype(BF16).astype(F32))
    k_inv[col + j, pl.ds(to_row, 1), :] = key_scale


def edge_kernel(side, feats, edge, sem):
    _, _, edge_row = halo_start(side)
    copy = pltpu.make_async_copy(feats.at[pl.ds(edge_row, 2)], edge, sem)
    copy.start()
    copy.wait()


def own_kernel(
    side, feats_hbm, cot_hbm, gain_hbm, w_q_hbm, w_kv_hbm, w_out_hbm,
    qs, ks, vs, ogs, q_inv, k_inv, normed, gain_out, w_in, w_back, feats, cot, w_q, w_kv, gain_row,
    w_out, sems,
):
    moves = (
        (gain_hbm, gain_row), (w_q_hbm, w_q), (w_kv_hbm, w_kv), (w_out_hbm, w_out),
        (feats_hbm, feats), (cot_hbm, cot),
    )
    copies = [pltpu.make_async_copy(a, b, sems.at[k]) for k, (a, b) in enumerate(moves)]
    for copy in copies:
        copy.start()
    _, clear_row, _ = halo_start(side)
    clear_rows((ks, vs), clear_row)
    clear_rows((qs, ogs), 0)
    clear_rows((qs, ogs), 10)
    for copy in copies[:4]:
        copy.wait()
    gain_col = jnp.sum(
        jnp.where(eye(), jnp.broadcast_to(gain_row[...], (CH, CH)), 0.0), axis=1, keepdims=True
    )
    gain_full = jnp.broadcast_to(gain_col, (CH, PIX))
    gain_out[...] = gain_full
    w_in[0:CH, :] = w_q[...].astype(F32).T.astype(BF16)
    w_in[CH:, :] = w_kv[...].astype(F32).T.astype(BF16)
    w_back[...] = jnp.concatenate([w_q[...].astype(F32), w_kv[...].astype(F32)], axis=1).astype(BF16)
    w_full = w_in[...]
    w_o = w_out[...]
    for copy in copies[4:]:
        copy.wait()

    def visit(row):
        views = normed_views(feats, row, gain_full)
        both = jnp.dot(w_full, jnp.concatenate(views, axis=1), preferred_element_type=F32)
        out_both = jnp.dot(w_o, pair(cot, row), preferred_element_type=F32)
        for j in range(2):
            normed[row, 2 + j] = views[j]
            raw = both[:, j * PIX : (j + 1) * PIX]
            query_scale = inv_rms(raw[:CH])
            put(qs, j, row + 2, (raw[:CH] * query_scale).astype(BF16).astype(F32))
            q_inv[j, pl.ds(row, 1), :] = query_scale
            project_keys(raw[CH:], row + 2, 2, j, ks, vs, k_inv)
            put(ogs, j, row + 2, out_both[:, j * PIX : (j + 1) * PIX])

    each_row(ROWS, (visit,))


def forward_kernel(
    side, first, second, row_halo, first_corner, second_corner, gain, w_in, ogs, qs,
    ks_in, vs_in, k_inv_in, normed_in,
    ks, vs, k_inv, normed, weights, prob_grads, attended, stats,
):
    halo_row, _, _ = halo_start(side)
    first_col, second_col = partner_cols(side)
    gain_full = gain[...]
    w_keys = w_in[CH:, :]

    def piece(ref, offset, to_row, col):
        def one(row):
            views = normed_views(ref, row, gain_full)
            both = jnp.dot(w_keys, jnp.concatenate(views, axis=1), preferred_element_type=F32)
            for j in range(2):
                normed[row + to_row, col + j] = views[j]
                project_keys(both[:, j * PIX : (j + 1) * PIX], row + offset, col, j, ks, vs, k_inv)

        return one

    each_row(ROWS, (piece(first, 2, 0, first_col), piece(second, 2, 0, second_col)))
    each_row(
        2,
        (
            piece(row_halo, halo_row, ROWS, 2),
            piece(first_corner, halo_row, ROWS, first_col),
            piece(second_corner, halo_row, ROWS, second_col),
        ),
    )

    def attend(step, carry):
        col, head = step // HEADS, step % HEADS
        base = head * (SIZE * S)
        query = [take(qs, col, base + d * S + 2) * SCALE for d in range(SIZE)]
        og = [take(ogs, col, base + d * S + 2) for d in range(SIZE)]
        acc = [jnp.zeros((ROWS, PIX), F32)] * SIZE
        exp_total = jnp.zeros((ROWS, PIX), F32)
        spread = jnp.zeros((ROWS, PIX), F32)
        for j in range(5):
            for i in range(5):
                key = [take(ks, col + j, base + d * S + i) for d in range(SIZE)]
                weight = jnp.exp(total(a * b for a, b in zip(query, key)))
                value = [take(vs, col + j, base + d * S + i) for d in range(SIZE)]
                prob_grad = total(a * b for a, b in zip(og, value))
                acc = [a + weight * b for a, b in zip(acc, value)]
                exp_total = exp_total + weight
                spread = spread + weight * prob_grad
                weights[step, 5 * j + i] = weight
                prob_grads[step, 5 * j + i] = prob_grad
        inv_total = 1.0 / exp_total
        for d in range(SIZE):
            attended[col, pl.ds((head * SIZE + d) * R, ROWS), :] = acc[d] * inv_total
        stats[0, step] = inv_total
        stats[1, step] = spread * inv_total
        return carry

    lax.fori_loop(0, COLS * HEADS, attend, 0)


def unit_back(unit, scale, upstream):
    mean = jnp.sum(upstream * unit, axis=0, keepdims=True) * (1.0 / CH)
    return scale[None] * (upstream - unit * mean)


def window(ref, col, row):
    return jnp.stack([take(ref, col, d * S + row) for d in range(CH)], axis=0)


def outer(left, right):
    return lax.dot_general(left, right, (((1,), (1,)), ((), ())), preferred_element_type=F32)


def view(ref, col, row, channels):
    return ref[col, pl.ds(row, channels, stride=R), :].astype(BF16)


def gradient_kernel(
    side, qs, ks, ogs, q_inv, k_inv, normed, weights, prob_grads, attended, stats, cot,
    weight_sums, raw_query, to_first, to_second, own_raw,
    probs, score_grads, grads, raws, halo_grads, halo_raws,
):
    _, _, edge_row = halo_start(side)
    first_col, second_col = partner_cols(side)
    zeros = jnp.zeros((ROWS, PIX), F32)
    pads = jnp.zeros((25, PIX), F32)

    def query_one(step, carry):
        col, head = step // HEADS, step % HEADS
        base = head * (SIZE * S)
        for ref in (probs, score_grads):
            for row in (0, 1, 10, 11):
                ref[step, pl.ds(row, 25, stride=W), :] = pads
        inv_total, spread = stats[0, step], stats[1, step]
        acc = [zeros] * SIZE
        for j in range(5):
            for i in range(5):
                o = 5 * j + i
                prob = weights[step, o] * inv_total
                score_grad = prob * (prob_grads[step, o] - spread)
                probs[step, pl.ds(o * W + 2, ROWS), :] = prob
                score_grads[step, pl.ds(o * W + 2, ROWS), :] = score_grad
                acc = [a + score_grad * take(ks, col + j, base + d * S + i) for d, a in enumerate(acc)]
        for d in range(SIZE):
            grads[col, head * SIZE + d] = acc[d]
        return carry

    lax.fori_loop(0, COLS * HEADS, query_one, 0)

    def query_finish(col, carry):
        raw = unit_back(window(qs, col, 2), q_inv[col] * SCALE, grads[col])
        for d in range(CH):
            raws[col, pl.ds(d * R, ROWS), :] = raw[d]
        return carry

    lax.fori_loop(0, COLS, query_finish, 0)

    def query_sums(half, carry):
        query_acc, out_acc = carry
        raw, mixed, normed_all, cot_all = [], [], [], []
        for row in (2 * half, 2 * half + 1):
            for j in range(2):
                raw.append(view(raws, j, row, CH))
                raw_query[row, j] = raw[-1]
                mixed.append(view(attended, j, row, CH))
                normed_all.append(normed[row, 2 + j])
                cot_all.append(cot[row, j])
        raw, mixed, normed_all, cot_all = (
            jnp.concatenate(x, axis=1) for x in (raw, mixed, normed_all, cot_all)
        )
        return query_acc + outer(normed_all, raw), out_acc + outer(mixed, cot_all)

    flat = jnp.zeros((CH, CH), F32)
    query_acc, out_acc = lax.fori_loop(0, ROWS // 2, query_sums, (flat, flat))
    weight_sums[CH : 2 * CH, :] = jnp.concatenate([query_acc, out_acc], axis=1)

    def key_step(acc, step, col, j, i, base, first_row):
        key_acc, value_acc = acc
        start = first_row - i + 2
        prob = probs[step, pl.ds((5 * j + i) * W + start, ROWS), :]
        score_grad = score_grads[step, pl.ds((5 * j + i) * W + start, ROWS), :]
        key_acc = [a + score_grad * take(qs, col, base + d * S + start) for d, a in enumerate(key_acc)]
        value_acc = [a + prob * take(ogs, col, base + d * S + start) for d, a in enumerate(value_acc)]
        return key_acc, value_acc

    edge_first, edge_offset = edge_row * 2 // 3, edge_row // 2

    def key_columns(view_col, head, cols):
        base = head * (SIZE * S)
        own_steps = [(i, 2) for i in range(5)]
        halo_steps = [(edge_offset + i, edge_first) for i in range(2)]
        for steps, key_ref, value_ref in (
            (own_steps, grads, raws), (halo_steps, halo_grads, halo_raws)
        ):
            acc = ([zeros] * SIZE, [zeros] * SIZE)
            for col in cols:
                for i, first_row in steps:
                    acc = key_step(acc, col * HEADS + head, col, view_col - col, i, base, first_row)
            for d in range(SIZE):
                key_ref[view_col, head * SIZE + d] = acc[0][d]
                value_ref[view_col, pl.ds((CH + head * SIZE + d) * R, ROWS), :] = acc[1][d]

    def inner_columns(step, carry):
        key_columns(1 + step // HEADS, step % HEADS, (0, 1))
        return carry

    def outer_columns(step, carry):
        side_col = step // HEADS
        key_columns(5 * side_col, step % HEADS, (side_col,))
        return carry

    lax.fori_loop(0, 4 * HEADS, inner_columns, 0)
    lax.fori_loop(0, 2 * HEADS, outer_columns, 0)

    def key_finish(col, carry):
        for source, target, row in ((grads, raws, 2), (halo_grads, halo_raws, edge_first)):
            scale = k_inv[col, pl.ds(row, ROWS), :] * SCALE
            raw = unit_back(window(ks, col, row), scale, source[col])
            for d in range(CH):
                target[col, pl.ds(d * R, ROWS), :] = raw[d]
        return carry

    lax.fori_loop(0, 6, key_finish, 0)

    def key_sums(source, from_row, first):
        def one(row, acc):
            raw, normed_all = [], []
            for target, col in ((to_first, first_col), (own_raw, 2), (to_second, second_col)):
                for j in range(2):
                    raw.append(view(source, col + j, row + from_row, 2 * CH))
                    target[row + first, j] = raw[-1]
                    normed_all.append(normed[row + first, col + j])
            return acc + outer(jnp.concatenate(normed_all, axis=1), jnp.concatenate(raw, axis=1))

        return one

    acc = lax.fori_loop(0, ROWS, key_sums(raws, 0, 0), jnp.zeros((CH, 2 * CH), F32))
    weight_sums[0:CH, :] = lax.fori_loop(0, 2, key_sums(halo_raws, edge_row, ROWS), acc)


def row_kernel(own_raw, first_raw, second_raw, row_send, parts, sems):
    copies = [
        pltpu.make_async_copy(x.at[pl.ds(ROWS, 2)], parts.at[k], sems.at[k])
        for k, x in enumerate((first_raw, second_raw))
    ]
    for copy in copies:
        copy.start()
    for copy in copies:
        copy.wait()
    for row in range(2):
        for j in range(2):
            row_send[row, j] = (
                own_raw[ROWS + row, j].astype(F32)
                + parts[0, row, j].astype(F32)
                + parts[1, row, j].astype(F32)
            ).astype(BF16)


def features_kernel(
    side, own_raw, first_raw, second_raw, row_raw, raw_query, feats, cot, gain, w_back,
    feats_grad, shared,
):
    _, _, edge_row = halo_start(side)

    def join(row):
        for j in range(2):
            shared[row, j] = (
                own_raw[row, j].astype(F32) + first_raw[row, j].astype(F32)
                + second_raw[row, j].astype(F32)
            )

    def join_edge(row):
        for j in range(2):
            shared[row + edge_row, j] = shared[row + edge_row, j] + row_raw[row, j].astype(F32)

    each_row(ROWS, (join,))
    each_row(2, (join_edge,))
    gain_full = gain[...]
    w_b = w_back[...]

    def view_row(row):
        raw = jnp.concatenate([pair(raw_query, row), pair(shared, row).astype(BF16)], axis=0)
        normed_grad = jnp.dot(w_b, raw, preferred_element_type=F32)
        for j in range(2):
            values = feats[row, j].astype(F32)
            inv_norm = inv_rms(values)
            scaled = values * inv_norm
            scaled_grad = normed_grad[:, j * PIX : (j + 1) * PIX] * gain_full
            mean = jnp.mean(scaled_grad * scaled, axis=0, keepdims=True)
            branch = inv_norm * (scaled_grad - scaled * mean)
            feats_grad[row, j] = (cot[row, j].astype(F32) + branch).astype(BF16)

    each_row(ROWS, (view_row,))


def last_kernel(factor, sums, w_q, w_kv, gain, query_grad, keyval_grad, output_grad, gain_grad):
    keyval = sums[0:CH, :] * factor
    rest = sums[CH : 2 * CH, :] * factor
    query = rest[:, :CH]
    keyval_grad[...] = keyval
    query_grad[...] = query
    output_grad[...] = rest[:, CH:]
    col = jnp.sum(query * w_q[...].astype(F32), axis=1, keepdims=True) + jnp.sum(
        keyval * w_kv[...].astype(F32), axis=1, keepdims=True
    )
    line = jnp.sum(jnp.where(eye(), jnp.broadcast_to(col, (CH, CH)), 0.0), axis=0, keepdims=True)
    gain_grad[...] = line / gain[...]


def call(kernel, outs, scratch, flops, *operands, aliases=(), far=()):
    return pl.pallas_call(
        kernel,
        out_shape=[jax.ShapeDtypeStruct(shape, dtype) for shape, dtype in outs],
        in_specs=[
            SM if x.dtype == jnp.int32 else FAR if k in far else VM for k, x in enumerate(operands)
        ],
        out_specs=[VM] * len(outs),
        scratch_shapes=[pltpu.VMEM(x, F32) if isinstance(x, tuple) else x for x in scratch],
        input_output_aliases=dict(aliases),
        compiler_params=pltpu.CompilerParams(vmem_limit_bytes=20 * 1024 * 1024),
        cost_estimate=pl.CostEstimate(flops=flops, bytes_accessed=1000000, transcendentals=0),
    )(*operands)


def near_memory(x):
    return pltpu.with_memory_space_constraint(x, pltpu.VMEM)


def sum_kernel(shares, copies):
    share = jnp.sum(shares[...].astype(F32), axis=0).astype(copies.dtype)
    for k in range(copies.shape[0]):
        copies[k] = share


def sum_everywhere(values):
    near, far = ("px", "pc", "vrow"), ("py", "vcol")
    near_count, far_count = (math.prod(lax.axis_size(a) for a in axes) for axes in (near, far))
    size = values.size // (near_count * PIX)

    def exchange(copies, axes):
        return near_memory(lax.all_to_all(copies, axes, 0, 0))

    shares = exchange(values.reshape(near_count, size, PIX), near)
    (copies,) = call(sum_kernel, [((far_count, size, PIX), BF16)], [], 100000, shares)
    shares = exchange(copies, far)
    (copies,) = call(sum_kernel, [((near_count, size, PIX), F32)], [], 100000, shares)
    return lax.all_to_all(copies, near, 0, 0).reshape(values.shape)


def layer(features, out_cotangent, norm_gain, query_proj, keyval_proj, output_proj):
    place = lax.axis_index("vrow") * 2 + jnp.bitwise_and(lax.axis_index("vcol"), 1)
    side = place.astype(jnp.int32).reshape(1)
    cols = lax.axis_size("vcol")
    grid = ("vrow", "vcol")

    def both_ways(pairs):
        return [*pairs, *((b, a) for a, b in pairs)]

    rounds = [[(i, i + 1) for i in range(start, cols - 1, 2)] for start in (0, 1)]
    first_swap, second_swap = (both_ways(pairs) for pairs in rounds)
    first_cross, second_cross = (
        [(a * cols + i, (1 - a) * cols + j) for a in (0, 1) for i, j in swap]
        for swap in (first_swap, second_swap)
    )
    row_swap = both_ways([(0, 1)])
    gain = norm_gain.reshape(1, CH)
    held = [
        pltpu.with_memory_space_constraint(x, pltpu.HBM)
        for x in (features, out_cotangent, gain, query_proj, keyval_proj, output_proj)
    ]

    (edge,) = call(
        edge_kernel, [((2, COLS, CH, PIX), BF16)], [pltpu.SemaphoreType.DMA], 1000, side, held[0],
        far=(1,),
    )
    first_corner = lax.ppermute(edge, grid, first_cross)
    second_corner = lax.ppermute(edge, grid, second_cross)
    first = lax.ppermute(features, "vcol", first_swap)
    second = lax.ppermute(features, "vcol", second_swap)
    row_halo = lax.ppermute(edge, "vrow", row_swap)

    own = ((COLS, CH * S, PIX), F32)
    padded = ((6, CH * S, PIX), F32)
    lanes = ((COLS, ROWS, PIX), F32)
    key_lanes = ((6, 16, PIX), F32)
    steps = COLS * HEADS
    offsets = ((steps, 25, ROWS, PIX), F32)
    views = ((ROWS, COLS, CH, PIX), BF16)
    all_views = ((ROWS + 2, 6, CH, PIX), BF16)
    key_views = ((ROWS + 2, COLS, 2 * CH, PIX), BF16)
    (
        qs, ks, vs, ogs, q_inv, k_inv, normed, gain_full, w_in, w_back, feats, cot, w_q, w_kv, gain_row,
    ) = call(
        own_kernel,
        [
            own, padded, padded, own, lanes, key_lanes, all_views, ((CH, PIX), F32),
            ((3 * CH, CH), BF16), ((CH, 3 * CH), BF16), views, views, ((CH, CH), BF16),
            ((CH, 2 * CH), BF16), ((1, CH), F32),
        ],
        [pltpu.VMEM((CH, CH), BF16), pltpu.SemaphoreType.DMA((6,))], 2000000,
        side, *held, far=(1, 2, 3, 4, 5, 6),
    )
    ks, vs, k_inv, normed, weights, prob_grads, attended, stats = call(
        forward_kernel,
        [
            padded, padded, key_lanes, all_views, offsets, offsets,
            ((COLS, CH * R, PIX), F32), ((2, steps, ROWS, PIX), F32),
        ],
        [], 4000000,
        side, first, second, row_halo, first_corner, second_corner, gain_full, w_in, ogs, qs,
        ks, vs, k_inv, normed,
        aliases=((10, 0), (11, 1), (12, 2), (13, 3)),
    )
    weight_sums, raw_query, to_first, to_second, own_raw = call(
        gradient_kernel,
        [((2 * CH, PIX), F32), views, key_views, key_views, key_views],
        [
            (steps, 25 * W, PIX), (steps, 25 * W, PIX), (6, CH, ROWS, PIX), (6, 2 * CH * R, PIX),
            (6, CH, ROWS, PIX), (6, 2 * CH * R, PIX),
        ],
        5000000,
        side, qs, ks, ogs, q_inv, k_inv, normed, weights, prob_grads, attended, stats, cot,
    )
    sums = sum_everywhere(weight_sums)
    first_raw, second_raw = (
        lax.ppermute(pltpu.with_memory_space_constraint(x, pltpu.HBM), "vcol", swap)
        for x, swap in ((to_first, first_swap), (to_second, second_swap))
    )
    (row_send,) = call(
        row_kernel, [((2, COLS, 2 * CH, PIX), BF16)],
        [pltpu.VMEM((2, 2, COLS, 2 * CH, PIX), BF16), pltpu.SemaphoreType.DMA((2,))], 10000,
        own_raw, first_raw, second_raw, far=(1, 2),
    )
    row_raw = lax.ppermute(row_send, "vrow", row_swap)
    (features_grad,) = call(
        features_kernel, [(features.shape, BF16)], [(ROWS, COLS, 2 * CH, PIX)], 2000000,
        side, own_raw, first_raw, second_raw, row_raw, raw_query, feats, cot, gain_full, w_back,
    )
    tokens_all = ROWS * COLS * PIX * math.prod(lax.axis_size(a) for a in AXES)
    query_grad, keyval_grad, output_grad, gain_grad = call(
        functools.partial(last_kernel, 1.0 / math.sqrt(tokens_all)),
        [((CH, CH), F32), ((CH, 2 * CH), F32), ((CH, CH), F32), ((1, CH), F32)],
        [], 100000,
        sums, w_q, w_kv, gain_row,
    )
    return features_grad, query_grad, keyval_grad, output_grad, gain_grad.reshape(CH)


def solution(mesh):
    rows, cols, _ = mesh.devices.shape
    parts = jax.sharding.Mesh(mesh.devices.reshape(rows, cols, 4, 4, 2), AXES)
    placed = P("vrow", "vcol", None, AXES[2:])
    return jax.shard_map(
        layer,
        mesh=parts,
        in_specs=(placed, placed, P(), P(), P(), P()),
        out_specs=(placed, P(), P(), P(), P()),
        check_vma=False,
    )
```

```python
import functools
import math

import jax
import jax.numpy as jnp
from jax import lax
from jax.experimental import pallas as pl
from jax.experimental.pallas import tpu as pltpu
from jax.sharding import PartitionSpec as P


AXES = ("vrow", "vcol", "px", "py", "pc")
HEADS = 4
SIZE = 16
CH = 64
ROWS = 8
COLS = 2
PIX = 128
S = 13
W = 13
R = 9
EPSILON = 1e-06
SCALE = SIZE ** (-0.5)
F32 = jnp.float32
BF16 = jnp.bfloat16

VM = pl.BlockSpec(memory_space=pltpu.VMEM)
FAR = pl.BlockSpec(memory_space=pltpu.HBM)
SM = pl.BlockSpec(memory_space=pltpu.SMEM)


def inv_rms(values):
    return lax.rsqrt(jnp.mean(values * values, axis=0, keepdims=True) + EPSILON)


def total(terms):
    terms = list(terms)
    while len(terms) > 1:
        terms = [a + b for a, b in zip(terms[::2], terms[1::2])] + (
            [terms[-1]] if len(terms) % 2 else []
        )
    return terms[0]


def put(ref, col, row, values):
    ref[col, pl.ds(row, values.shape[0], stride=S), :] = values


def take(ref, col, start):
    return ref[col, pl.ds(start, ROWS), :]


def pair(ref, row, first=0):
    return jnp.concatenate([ref[row, first], ref[row, first + 1]], axis=1)


def each_row(count, visits):
    def one(row, carry):
        for visit in visits:
            visit(row)
        return carry

    lax.fori_loop(0, count, one, 0)


def halo_start(side_ref):
    side = jnp.right_shift(side_ref[0], 1)
    return 10 - 10 * side, 10 * side, 6 - 6 * side


def partner_cols(side_ref):
    odd = jnp.bitwise_and(side_ref[0], 1)
    return 4 - 4 * odd, 4 * odd


def clear_rows(refs, row):
    for ref in refs:
        zeros = jnp.zeros((ref.shape[1] // S, PIX), F32)
        for col in range(ref.shape[0]):
            put(ref, col, row, zeros)
            put(ref, col, row + 1, zeros)


def eye():
    shape = (CH, CH)
    return lax.broadcasted_iota(jnp.int32, shape, 0) == lax.broadcasted_iota(jnp.int32, shape, 1)


def normed_views(ref, row, gain):
    out = []
    for j in range(2):
        values = ref[row, j].astype(F32)
        out.append((values * inv_rms(values) * gain).astype(BF16))
    return out


def project_keys(raw, to_row, col, j, ks, vs, k_inv):
    key, value = raw[:CH], raw[CH:]
    key_scale = inv_rms(key)
    put(ks, col + j, to_row, (key * key_scale).astype(BF16).astype(F32))
    put(vs, col + j, to_row, value.astype(BF16).astype(F32))
    k_inv[col + j, pl.ds(to_row, 1), :] = key_scale


def fetch_kernel(
    side, feats_hbm, cot_hbm, gain_hbm, w_q_hbm, w_kv_hbm, w_out_hbm,
    edge, feats, cot, gain_row, w_q, w_kv, w_out, sems,
):
    _, _, edge_row = halo_start(side)
    moves = (
        (feats_hbm.at[pl.ds(edge_row, 2)], edge), (feats_hbm, feats), (cot_hbm, cot),
        (gain_hbm, gain_row), (w_q_hbm, w_q), (w_kv_hbm, w_kv), (w_out_hbm, w_out),
    )
    copies = [pltpu.make_async_copy(a, b, sems.at[k]) for k, (a, b) in enumerate(moves)]
    for copy in copies:
        copy.start()
    for copy in copies:
        copy.wait()


def own_kernel(
    side, feats, cot, gain_row, w_q, w_kv, w_out,
    qs, ks, vs, ogs, q_inv, k_inv, normed, gain_out, w_in, w_back,
):
    _, clear_row, _ = halo_start(side)
    clear_rows((ks, vs), clear_row)
    clear_rows((qs, ogs), 0)
    clear_rows((qs, ogs), 10)
    gain_col = jnp.sum(
        jnp.where(eye(), jnp.broadcast_to(gain_row[...], (CH, CH)), 0.0), axis=1, keepdims=True
    )
    gain_full = jnp.broadcast_to(gain_col, (CH, PIX))
    gain_out[...] = gain_full
    w_in[0:CH, :] = w_q[...].astype(F32).T.astype(BF16)
    w_in[CH:, :] = w_kv[...].astype(F32).T.astype(BF16)
    w_back[...] = jnp.concatenate([w_q[...].astype(F32), w_kv[...].astype(F32)], axis=1).astype(BF16)
    w_full = w_in[...]
    w_o = w_out[...]

    def visit(row):
        views = normed_views(feats, row, gain_full)
        both = jnp.dot(w_full, jnp.concatenate(views, axis=1), preferred_element_type=F32)
        out_both = jnp.dot(w_o, pair(cot, row), preferred_element_type=F32)
        for j in range(2):
            normed[row, 2 + j] = views[j]
            raw = both[:, j * PIX : (j + 1) * PIX]
            query_scale = inv_rms(raw[:CH])
            put(qs, j, row + 2, (raw[:CH] * query_scale).astype(BF16).astype(F32))
            q_inv[j, pl.ds(row, 1), :] = query_scale
            project_keys(raw[CH:], row + 2, 2, j, ks, vs, k_inv)
            put(ogs, j, row + 2, out_both[:, j * PIX : (j + 1) * PIX])

    each_row(ROWS, (visit,))


def forward_kernel(
    side, first, second, row_halo, first_corner, second_corner, gain, w_in, ogs, qs,
    ks_in, vs_in, k_inv_in, normed_in,
    ks, vs, k_inv, normed, weights, prob_grads, attended, stats,
):
    halo_row, _, _ = halo_start(side)
    first_col, second_col = partner_cols(side)
    gain_full = gain[...]
    w_keys = w_in[CH:, :]

    def piece(ref, offset, to_row, col):
        def one(row):
            views = normed_views(ref, row, gain_full)
            both = jnp.dot(w_keys, jnp.concatenate(views, axis=1), preferred_element_type=F32)
            for j in range(2):
                normed[row + to_row, col + j] = views[j]
                project_keys(both[:, j * PIX : (j + 1) * PIX], row + offset, col, j, ks, vs, k_inv)

        return one

    each_row(ROWS, (piece(first, 2, 0, first_col), piece(second, 2, 0, second_col)))
    each_row(
        2,
        (
            piece(row_halo, halo_row, ROWS, 2),
            piece(first_corner, halo_row, ROWS, first_col),
            piece(second_corner, halo_row, ROWS, second_col),
        ),
    )

    def attend(step, carry):
        col, head = step // HEADS, step % HEADS
        base = head * (SIZE * S)
        query = [take(qs, col, base + d * S + 2) * SCALE for d in range(SIZE)]
        og = [take(ogs, col, base + d * S + 2) for d in range(SIZE)]
        acc = [jnp.zeros((ROWS, PIX), F32)] * SIZE
        exp_total = jnp.zeros((ROWS, PIX), F32)
        spread = jnp.zeros((ROWS, PIX), F32)
        for j in range(5):
            for i in range(5):
                key = [take(ks, col + j, base + d * S + i) for d in range(SIZE)]
                weight = jnp.exp(total(a * b for a, b in zip(query, key)))
                value = [take(vs, col + j, base + d * S + i) for d in range(SIZE)]
                prob_grad = total(a * b for a, b in zip(og, value))
                acc = [a + weight * b for a, b in zip(acc, value)]
                exp_total = exp_total + weight
                spread = spread + weight * prob_grad
                weights[step, 5 * j + i] = weight
                prob_grads[step, 5 * j + i] = prob_grad
        inv_total = 1.0 / exp_total
        for d in range(SIZE):
            attended[col, pl.ds((head * SIZE + d) * R, ROWS), :] = acc[d] * inv_total
        stats[0, step] = inv_total
        stats[1, step] = spread * inv_total
        return carry

    lax.fori_loop(0, COLS * HEADS, attend, 0)


def unit_back(unit, scale, upstream):
    mean = jnp.sum(upstream * unit, axis=0, keepdims=True) * (1.0 / CH)
    return scale[None] * (upstream - unit * mean)


def window(ref, col, row):
    return jnp.stack([take(ref, col, d * S + row) for d in range(CH)], axis=0)


def outer(left, right):
    return lax.dot_general(left, right, (((1,), (1,)), ((), ())), preferred_element_type=F32)


def view(ref, col, row, channels):
    return ref[col, pl.ds(row, channels, stride=R), :].astype(BF16)


def gradient_kernel(
    side, qs, ks, ogs, q_inv, k_inv, normed, weights, prob_grads, attended, stats, cot,
    weight_sums, raw_query, to_first, to_second, own_raw,
    probs, score_grads, grads, raws, halo_grads, halo_raws,
):
    _, _, edge_row = halo_start(side)
    first_col, second_col = partner_cols(side)
    zeros = jnp.zeros((ROWS, PIX), F32)
    pads = jnp.zeros((25, PIX), F32)

    def query_one(step, carry):
        col, head = step // HEADS, step % HEADS
        base = head * (SIZE * S)
        for ref in (probs, score_grads):
            for row in (0, 1, 10, 11):
                ref[step, pl.ds(row, 25, stride=W), :] = pads
        inv_total, spread = stats[0, step], stats[1, step]
        acc = [zeros] * SIZE
        for j in range(5):
            for i in range(5):
                o = 5 * j + i
                prob = weights[step, o] * inv_total
                score_grad = prob * (prob_grads[step, o] - spread)
                probs[step, pl.ds(o * W + 2, ROWS), :] = prob
                score_grads[step, pl.ds(o * W + 2, ROWS), :] = score_grad
                acc = [a + score_grad * take(ks, col + j, base + d * S + i) for d, a in enumerate(acc)]
        for d in range(SIZE):
            grads[col, head * SIZE + d] = acc[d]
        return carry

    lax.fori_loop(0, COLS * HEADS, query_one, 0)

    def query_finish(col, carry):
        raw = unit_back(window(qs, col, 2), q_inv[col] * SCALE, grads[col])
        for d in range(CH):
            raws[col, pl.ds(d * R, ROWS), :] = raw[d]
        return carry

    lax.fori_loop(0, COLS, query_finish, 0)

    def query_sums(half, carry):
        query_acc, out_acc = carry
        raw, mixed, normed_all, cot_all = [], [], [], []
        for row in (2 * half, 2 * half + 1):
            for j in range(2):
                raw.append(view(raws, j, row, CH))
                raw_query[row, j] = raw[-1]
                mixed.append(view(attended, j, row, CH))
                normed_all.append(normed[row, 2 + j])
                cot_all.append(cot[row, j])
        raw, mixed, normed_all, cot_all = (
            jnp.concatenate(x, axis=1) for x in (raw, mixed, normed_all, cot_all)
        )
        return query_acc + outer(normed_all, raw), out_acc + outer(mixed, cot_all)

    flat = jnp.zeros((CH, CH), F32)
    query_acc, out_acc = lax.fori_loop(0, ROWS // 2, query_sums, (flat, flat))
    weight_sums[CH : 2 * CH, :] = jnp.concatenate([query_acc, out_acc], axis=1)

    edge_first, edge_offset = edge_row * 2 // 3, edge_row // 2

    def key_columns(view_cols, channel, count, head, cols):
        own_steps = [(i, 2) for i in range(5)]
        halo_steps = [(edge_offset + i, edge_first) for i in range(2)]
        for steps, key_ref, value_ref in (
            (own_steps, grads, raws), (halo_steps, halo_grads, halo_raws)
        ):
            key_acc = [[zeros] * count for _ in view_cols]
            value_acc = [[zeros] * count for _ in view_cols]
            for col in cols:
                for i, first_row in steps:
                    start = first_row - i + 2
                    query = [take(qs, col, (channel + d) * S + start) for d in range(count)]
                    og = [take(ogs, col, (channel + d) * S + start) for d in range(count)]
                    for k, view_col in enumerate(view_cols):
                        row = (5 * (view_col - col) + i) * W + start
                        prob = probs[col * HEADS + head, pl.ds(row, ROWS), :]
                        score_grad = score_grads[col * HEADS + head, pl.ds(row, ROWS), :]
                        key_acc[k] = [a + score_grad * b for a, b in zip(key_acc[k], query)]
                        value_acc[k] = [a + prob * b for a, b in zip(value_acc[k], og)]
            for k, view_col in enumerate(view_cols):
                for d in range(count):
                    key_ref[view_col, channel + d] = key_acc[k][d]
                    value_ref[view_col, pl.ds((CH + channel + d) * R, ROWS), :] = value_acc[k][d]

    half = SIZE // 2

    def inner_columns(step, carry):
        first, part = 1 + step // (2 * HEADS) * 2, step % (2 * HEADS)
        key_columns((first, first + 1), part * half, half, part // 2, (0, 1))
        return carry

    def outer_columns(step, carry):
        side_col, head = step // HEADS, step % HEADS
        key_columns((5 * side_col,), head * SIZE, SIZE, head, (side_col,))
        return carry

    lax.fori_loop(0, 4 * HEADS, inner_columns, 0)
    lax.fori_loop(0, 2 * HEADS, outer_columns, 0)

    def key_finish(col, carry):
        for source, target, row in ((grads, raws, 2), (halo_grads, halo_raws, edge_first)):
            scale = k_inv[col, pl.ds(row, ROWS), :] * SCALE
            raw = unit_back(window(ks, col, row), scale, source[col])
            for d in range(CH):
                target[col, pl.ds(d * R, ROWS), :] = raw[d]
        return carry

    lax.fori_loop(0, 6, key_finish, 0)

    def key_sums(source, from_row, first):
        def one(row, acc):
            raw, normed_all = [], []
            for target, col in ((to_first, first_col), (own_raw, 2), (to_second, second_col)):
                for j in range(2):
                    raw.append(view(source, col + j, row + from_row, 2 * CH))
                    target[row + first, j] = raw[-1]
                    normed_all.append(normed[row + first, col + j])
            return acc + outer(jnp.concatenate(normed_all, axis=1), jnp.concatenate(raw, axis=1))

        return one

    acc = lax.fori_loop(0, ROWS, key_sums(raws, 0, 0), jnp.zeros((CH, 2 * CH), F32))
    weight_sums[0:CH, :] = lax.fori_loop(0, 2, key_sums(halo_raws, edge_row, ROWS), acc)


def row_kernel(own_raw, first_raw, second_raw, row_send, parts, sems):
    copies = [
        pltpu.make_async_copy(x.at[pl.ds(ROWS, 2)], parts.at[k], sems.at[k])
        for k, x in enumerate((first_raw, second_raw))
    ]
    for copy in copies:
        copy.start()
    for copy in copies:
        copy.wait()
    for row in range(2):
        for j in range(2):
            row_send[row, j] = (
                own_raw[ROWS + row, j].astype(F32)
                + parts[0, row, j].astype(F32)
                + parts[1, row, j].astype(F32)
            ).astype(BF16)


def features_kernel(
    side, own_raw, first_raw, second_raw, row_raw, raw_query, feats, cot, gain, w_back,
    feats_grad, shared, query_part, parts, sems,
):
    copies = [
        pltpu.make_async_copy(x.at[pl.ds(0, ROWS)], parts.at[k], sems.at[k])
        for k, x in enumerate((first_raw, second_raw))
    ]
    for copy in copies:
        copy.start()
    _, _, edge_row = halo_start(side)
    gain_full = gain[...]
    w_query, w_keys = w_back[:, :CH], w_back[:, CH:]

    def query_row(row):
        query_part[row] = jnp.dot(w_query, pair(raw_query, row), preferred_element_type=F32)

    each_row(ROWS, (query_row,))
    for copy in copies:
        copy.wait()

    def join(row):
        for j in range(2):
            shared[row, j] = (
                own_raw[row, j].astype(F32) + parts[0, row, j].astype(F32)
                + parts[1, row, j].astype(F32)
            )

    def join_edge(row):
        for j in range(2):
            shared[row + edge_row, j] = shared[row + edge_row, j] + row_raw[row, j].astype(F32)

    each_row(ROWS, (join,))
    each_row(2, (join_edge,))

    def view_row(row):
        raw = pair(shared, row).astype(BF16)
        normed_grad = query_part[row] + jnp.dot(w_keys, raw, preferred_element_type=F32)
        for j in range(2):
            values = feats[row, j].astype(F32)
            inv_norm = inv_rms(values)
            scaled = values * inv_norm
            scaled_grad = normed_grad[:, j * PIX : (j + 1) * PIX] * gain_full
            mean = jnp.mean(scaled_grad * scaled, axis=0, keepdims=True)
            branch = inv_norm * (scaled_grad - scaled * mean)
            feats_grad[row, j] = (cot[row, j].astype(F32) + branch).astype(BF16)

    each_row(ROWS, (view_row,))


def last_kernel(factor, sums, w_q, w_kv, gain, query_grad, keyval_grad, output_grad, gain_grad):
    keyval = sums[0:CH, :] * factor
    rest = sums[CH : 2 * CH, :] * factor
    query = rest[:, :CH]
    keyval_grad[...] = keyval
    query_grad[...] = query
    output_grad[...] = rest[:, CH:]
    col = jnp.sum(query * w_q[...].astype(F32), axis=1, keepdims=True) + jnp.sum(
        keyval * w_kv[...].astype(F32), axis=1, keepdims=True
    )
    line = jnp.sum(jnp.where(eye(), jnp.broadcast_to(col, (CH, CH)), 0.0), axis=0, keepdims=True)
    gain_grad[...] = line / gain[...]


def call(kernel, outs, scratch, flops, *operands, aliases=(), far=()):
    return pl.pallas_call(
        kernel,
        out_shape=[jax.ShapeDtypeStruct(shape, dtype) for shape, dtype in outs],
        in_specs=[
            SM if x.dtype == jnp.int32 else FAR if k in far else VM for k, x in enumerate(operands)
        ],
        out_specs=[VM] * len(outs),
        scratch_shapes=[pltpu.VMEM(x, F32) if isinstance(x, tuple) else x for x in scratch],
        input_output_aliases=dict(aliases),
        compiler_params=pltpu.CompilerParams(vmem_limit_bytes=20 * 1024 * 1024),
        cost_estimate=pl.CostEstimate(flops=flops, bytes_accessed=1000000, transcendentals=0),
    )(*operands)


def near_memory(x):
    return pltpu.with_memory_space_constraint(x, pltpu.VMEM)


def sum_kernel(shares, copies):
    share = jnp.sum(shares[...].astype(F32), axis=0).astype(copies.dtype)
    for k in range(copies.shape[0]):
        copies[k] = share


def sum_everywhere(values):
    near, far = ("px", "pc", "vrow"), ("py", "vcol")
    near_count, far_count = (math.prod(lax.axis_size(a) for a in axes) for axes in (near, far))
    size = values.size // (near_count * PIX)

    def exchange(copies, axes):
        return near_memory(lax.all_to_all(copies, axes, 0, 0))

    shares = exchange(values.reshape(near_count, size, PIX), near)
    (copies,) = call(sum_kernel, [((far_count, size, PIX), BF16)], [], 100000, shares)
    shares = exchange(copies, far)
    (copies,) = call(sum_kernel, [((near_count, size, PIX), F32)], [], 100000, shares)
    return lax.all_to_all(copies, near, 0, 0).reshape(values.shape)


def layer(features, out_cotangent, norm_gain, query_proj, keyval_proj, output_proj):
    place = lax.axis_index("vrow") * 2 + jnp.bitwise_and(lax.axis_index("vcol"), 1)
    side = place.astype(jnp.int32).reshape(1)
    cols = lax.axis_size("vcol")
    grid = ("vrow", "vcol")

    def both_ways(pairs):
        return [*pairs, *((b, a) for a, b in pairs)]

    rounds = [[(i, i + 1) for i in range(start, cols - 1, 2)] for start in (0, 1)]
    first_swap, second_swap = (both_ways(pairs) for pairs in rounds)
    first_cross, second_cross = (
        [(a * cols + i, (1 - a) * cols + j) for a in (0, 1) for i, j in swap]
        for swap in (first_swap, second_swap)
    )
    row_swap = both_ways([(0, 1)])
    gain = norm_gain.reshape(1, CH)
    held = [
        pltpu.with_memory_space_constraint(x, pltpu.HBM)
        for x in (features, out_cotangent, gain, query_proj, keyval_proj, output_proj)
    ]

    views = ((ROWS, COLS, CH, PIX), BF16)
    edge, feats, cot, gain_row, w_q, w_kv, w_out = call(
        fetch_kernel,
        [
            ((2, COLS, CH, PIX), BF16), views, views, ((1, CH), F32), ((CH, CH), BF16),
            ((CH, 2 * CH), BF16), ((CH, CH), BF16),
        ],
        [pltpu.SemaphoreType.DMA((7,))], 1000, side, *held, far=(1, 2, 3, 4, 5, 6),
    )
    first_corner = lax.ppermute(edge, grid, first_cross)
    second_corner = lax.ppermute(edge, grid, second_cross)
    first = lax.ppermute(features, "vcol", first_swap)
    second = lax.ppermute(features, "vcol", second_swap)
    row_halo = lax.ppermute(edge, "vrow", row_swap)

    own = ((COLS, CH * S, PIX), F32)
    padded = ((6, CH * S, PIX), F32)
    lanes = ((COLS, ROWS, PIX), F32)
    key_lanes = ((6, 16, PIX), F32)
    steps = COLS * HEADS
    offsets = ((steps, 25, ROWS, PIX), F32)
    all_views = ((ROWS + 2, 6, CH, PIX), BF16)
    key_views = ((ROWS + 2, COLS, 2 * CH, PIX), BF16)
    qs, ks, vs, ogs, q_inv, k_inv, normed, gain_full, w_in, w_back = call(
        own_kernel,
        [
            own, padded, padded, own, lanes, key_lanes, all_views, ((CH, PIX), F32),
            ((3 * CH, CH), BF16), ((CH, 3 * CH), BF16),
        ],
        [], 2000000,
        side, feats, cot, gain_row, w_q, w_kv, w_out,
    )
    ks, vs, k_inv, normed, weights, prob_grads, attended, stats = call(
        forward_kernel,
        [
            padded, padded, key_lanes, all_views, offsets, offsets,
            ((COLS, CH * R, PIX), F32), ((2, steps, ROWS, PIX), F32),
        ],
        [], 4000000,
        side, first, second, row_halo, first_corner, second_corner, gain_full, w_in, ogs, qs,
        ks, vs, k_inv, normed,
        aliases=((10, 0), (11, 1), (12, 2), (13, 3)),
    )
    weight_sums, raw_query, to_first, to_second, own_raw = call(
        gradient_kernel,
        [((2 * CH, PIX), F32), views, key_views, key_views, key_views],
        [
            (steps, 25 * W, PIX), (steps, 25 * W, PIX), (6, CH, ROWS, PIX), (6, 2 * CH * R, PIX),
            (6, CH, ROWS, PIX), (6, 2 * CH * R, PIX),
        ],
        5000000,
        side, qs, ks, ogs, q_inv, k_inv, normed, weights, prob_grads, attended, stats, cot,
    )
    sums = sum_everywhere(weight_sums)
    first_raw, second_raw = (
        lax.ppermute(pltpu.with_memory_space_constraint(x, pltpu.HBM), "vcol", swap)
        for x, swap in ((to_first, first_swap), (to_second, second_swap))
    )
    (row_send,) = call(
        row_kernel, [((2, COLS, 2 * CH, PIX), BF16)],
        [pltpu.VMEM((2, 2, COLS, 2 * CH, PIX), BF16), pltpu.SemaphoreType.DMA((2,))], 10000,
        own_raw, first_raw, second_raw, far=(1, 2),
    )
    row_raw = lax.ppermute(row_send, "vrow", row_swap)
    (features_grad,) = call(
        features_kernel, [(features.shape, BF16)],
        [
            (ROWS, COLS, 2 * CH, PIX), (ROWS, CH, COLS * PIX),
            pltpu.VMEM((2, ROWS, COLS, 2 * CH, PIX), BF16), pltpu.SemaphoreType.DMA((2,)),
        ],
        2000000,
        side, own_raw, first_raw, second_raw, row_raw, raw_query, feats, cot, gain_full, w_back,
        far=(2, 3),
    )
    tokens_all = ROWS * COLS * PIX * math.prod(lax.axis_size(a) for a in AXES)
    query_grad, keyval_grad, output_grad, gain_grad = call(
        functools.partial(last_kernel, 1.0 / math.sqrt(tokens_all)),
        [((CH, CH), F32), ((CH, 2 * CH), F32), ((CH, CH), F32), ((1, CH), F32)],
        [], 100000,
        sums, w_q, w_kv, gain_row,
    )
    return features_grad, query_grad, keyval_grad, output_grad, gain_grad.reshape(CH)


def solution(mesh):
    rows, cols, _ = mesh.devices.shape
    parts = jax.sharding.Mesh(mesh.devices.reshape(rows, cols, 4, 4, 2), AXES)
    placed = P("vrow", "vcol", None, AXES[2:])
    return jax.shard_map(
        layer,
        mesh=parts,
        in_specs=(placed, placed, P(), P(), P(), P()),
        out_specs=(placed, P(), P(), P(), P()),
        check_vma=False,
    )
```

```python
import functools
import math

import jax
import jax.numpy as jnp
from jax import lax
from jax.experimental import pallas as pl
from jax.experimental.pallas import tpu as pltpu
from jax.sharding import PartitionSpec as P


AXES = ("vrow", "vcol", "px", "py", "pc")
HEADS = 4
SIZE = 16
CH = 64
ROWS = 8
COLS = 2
PIX = 128
S = 13
W = 13
R = 9
EPSILON = 1e-06
SCALE = SIZE ** (-0.5)
F32 = jnp.float32
BF16 = jnp.bfloat16

VM = pl.BlockSpec(memory_space=pltpu.VMEM)
FAR = pl.BlockSpec(memory_space=pltpu.HBM)
SM = pl.BlockSpec(memory_space=pltpu.SMEM)


def inv_rms(values):
    return lax.rsqrt(jnp.mean(values * values, axis=0, keepdims=True) + EPSILON)


def total(terms):
    terms = list(terms)
    while len(terms) > 1:
        terms = [a + b for a, b in zip(terms[::2], terms[1::2])] + (
            [terms[-1]] if len(terms) % 2 else []
        )
    return terms[0]


def put(ref, col, row, values):
    ref[col, pl.ds(row, values.shape[0], stride=S), :] = values


def take(ref, col, start):
    return ref[col, pl.ds(start, ROWS), :]


def pair(ref, row, first=0):
    return jnp.concatenate([ref[row, first], ref[row, first + 1]], axis=1)


def each_row(count, visits):
    def one(row, carry):
        for visit in visits:
            visit(row)
        return carry

    lax.fori_loop(0, count, one, 0)


def halo_start(side_ref):
    side = jnp.right_shift(side_ref[0], 1)
    return 10 - 10 * side, 10 * side, 6 - 6 * side


def partner_cols(side_ref):
    odd = jnp.bitwise_and(side_ref[0], 1)
    return 4 - 4 * odd, 4 * odd


def clear_rows(refs, row):
    for ref in refs:
        zeros = jnp.zeros((ref.shape[1] // S, PIX), F32)
        for col in range(ref.shape[0]):
            put(ref, col, row, zeros)
            put(ref, col, row + 1, zeros)


def eye():
    shape = (CH, CH)
    return lax.broadcasted_iota(jnp.int32, shape, 0) == lax.broadcasted_iota(jnp.int32, shape, 1)


def normed_views(ref, row, gain):
    out = []
    for j in range(2):
        values = ref[row, j].astype(F32)
        out.append((values * inv_rms(values) * gain).astype(BF16))
    return out


def project_keys(raw, to_row, col, j, ks, vs, k_inv):
    key, value = raw[:CH], raw[CH:]
    key_scale = inv_rms(key)
    put(ks, col + j, to_row, (key * key_scale).astype(BF16).astype(F32))
    put(vs, col + j, to_row, value.astype(BF16).astype(F32))
    k_inv[col + j, pl.ds(to_row, 1), :] = key_scale


def fetch_kernel(
    side, feats_hbm, cot_hbm, gain_hbm, w_q_hbm, w_kv_hbm, w_out_hbm,
    edge, feats, cot, gain_row, w_q, w_kv, w_out, sems,
):
    _, _, edge_row = halo_start(side)
    moves = (
        (feats_hbm.at[pl.ds(edge_row, 2)], edge), (feats_hbm, feats), (cot_hbm, cot),
        (gain_hbm, gain_row), (w_q_hbm, w_q), (w_kv_hbm, w_kv), (w_out_hbm, w_out),
    )
    copies = [pltpu.make_async_copy(a, b, sems.at[k]) for k, (a, b) in enumerate(moves)]
    for copy in copies:
        copy.start()
    for copy in copies:
        copy.wait()


def own_kernel(
    side, feats, cot, gain_row, w_q, w_kv, w_out,
    qs, ks, vs, ogs, q_inv, k_inv, normed, gain_out, w_in, w_back,
):
    _, clear_row, _ = halo_start(side)
    clear_rows((ks, vs), clear_row)
    clear_rows((qs, ogs), 0)
    clear_rows((qs, ogs), 10)
    gain_col = jnp.sum(
        jnp.where(eye(), jnp.broadcast_to(gain_row[...], (CH, CH)), 0.0), axis=1, keepdims=True
    )
    gain_full = jnp.broadcast_to(gain_col, (CH, PIX))
    gain_out[...] = gain_full
    w_in[0:CH, :] = w_q[...].astype(F32).T.astype(BF16)
    w_in[CH:, :] = w_kv[...].astype(F32).T.astype(BF16)
    w_back[...] = jnp.concatenate([w_q[...].astype(F32), w_kv[...].astype(F32)], axis=1).astype(BF16)
    w_full = w_in[...]
    w_o = w_out[...]

    def visit(row):
        views = normed_views(feats, row, gain_full)
        both = jnp.dot(w_full, jnp.concatenate(views, axis=1), preferred_element_type=F32)
        out_both = jnp.dot(w_o, pair(cot, row), preferred_element_type=F32)
        for j in range(2):
            normed[row, 2 + j] = views[j]
            raw = both[:, j * PIX : (j + 1) * PIX]
            query_scale = inv_rms(raw[:CH])
            put(qs, j, row + 2, (raw[:CH] * query_scale).astype(BF16).astype(F32))
            q_inv[j, pl.ds(row, 1), :] = query_scale
            project_keys(raw[CH:], row + 2, 2, j, ks, vs, k_inv)
            put(ogs, j, row + 2, out_both[:, j * PIX : (j + 1) * PIX])

    each_row(ROWS, (visit,))


def forward_kernel(
    side, first, second, row_halo, first_corner, second_corner, gain, w_in, ogs, qs,
    ks_in, vs_in, k_inv_in, normed_in,
    ks, vs, k_inv, normed, weights, prob_grads, attended, stats,
):
    halo_row, _, _ = halo_start(side)
    first_col, second_col = partner_cols(side)
    gain_full = gain[...]
    w_keys = w_in[CH:, :]

    def piece(ref, offset, to_row, col):
        def one(row):
            views = normed_views(ref, row, gain_full)
            both = jnp.dot(w_keys, jnp.concatenate(views, axis=1), preferred_element_type=F32)
            for j in range(2):
                normed[row + to_row, col + j] = views[j]
                project_keys(both[:, j * PIX : (j + 1) * PIX], row + offset, col, j, ks, vs, k_inv)

        return one

    each_row(ROWS, (piece(first, 2, 0, first_col), piece(second, 2, 0, second_col)))
    each_row(
        2,
        (
            piece(row_halo, halo_row, ROWS, 2),
            piece(first_corner, halo_row, ROWS, first_col),
            piece(second_corner, halo_row, ROWS, second_col),
        ),
    )

    def attend(step, carry):
        col, head = step // HEADS, step % HEADS
        base = head * (SIZE * S)
        query = [take(qs, col, base + d * S + 2) * SCALE for d in range(SIZE)]
        og = [take(ogs, col, base + d * S + 2) for d in range(SIZE)]
        acc = [jnp.zeros((ROWS, PIX), F32)] * SIZE
        exp_total = jnp.zeros((ROWS, PIX), F32)
        spread = jnp.zeros((ROWS, PIX), F32)
        for j in range(5):
            for i in range(5):
                key = [take(ks, col + j, base + d * S + i) for d in range(SIZE)]
                weight = jnp.exp(total(a * b for a, b in zip(query, key)))
                value = [take(vs, col + j, base + d * S + i) for d in range(SIZE)]
                prob_grad = total(a * b for a, b in zip(og, value))
                acc = [a + weight * b for a, b in zip(acc, value)]
                exp_total = exp_total + weight
                spread = spread + weight * prob_grad
                weights[step, 5 * j + i] = weight
                prob_grads[step, 5 * j + i] = prob_grad
        inv_total = 1.0 / exp_total
        for d in range(SIZE):
            attended[col, pl.ds((head * SIZE + d) * R, ROWS), :] = acc[d] * inv_total
        stats[0, step] = inv_total
        stats[1, step] = spread * inv_total
        return carry

    lax.fori_loop(0, COLS * HEADS, attend, 0)


def unit_back(unit, scale, upstream):
    mean = jnp.sum(upstream * unit, axis=0, keepdims=True) * (1.0 / CH)
    return scale[None] * (upstream - unit * mean)


def window(ref, col, row):
    return jnp.stack([take(ref, col, d * S + row) for d in range(CH)], axis=0)


def outer(left, right):
    return lax.dot_general(left, right, (((1,), (1,)), ((), ())), preferred_element_type=F32)


def view(ref, col, row, channels):
    return ref[col, pl.ds(row, channels, stride=R), :].astype(BF16)


def gradient_kernel(
    side, qs, ks, ogs, q_inv, k_inv, normed, weights, prob_grads, attended, stats, cot, w_kv,
    weight_sums, raw_query, to_first, to_second, own_raw, own_edge,
    probs, score_grads, grads, raws, halo_grads, halo_raws,
):
    _, _, edge_row = halo_start(side)
    first_col, second_col = partner_cols(side)
    zeros = jnp.zeros((ROWS, PIX), F32)
    pads = jnp.zeros((25, PIX), F32)

    def query_one(step, carry):
        col, head = step // HEADS, step % HEADS
        base = head * (SIZE * S)
        for ref in (probs, score_grads):
            for row in (0, 1, 10, 11):
                ref[step, pl.ds(row, 25, stride=W), :] = pads
        inv_total, spread = stats[0, step], stats[1, step]
        acc = [zeros] * SIZE
        for j in range(5):
            for i in range(5):
                o = 5 * j + i
                prob = weights[step, o] * inv_total
                score_grad = prob * (prob_grads[step, o] - spread)
                probs[step, pl.ds(o * W + 2, ROWS), :] = prob
                score_grads[step, pl.ds(o * W + 2, ROWS), :] = score_grad
                acc = [a + score_grad * take(ks, col + j, base + d * S + i) for d, a in enumerate(acc)]
        for d in range(SIZE):
            grads[col, head * SIZE + d] = acc[d]
        return carry

    lax.fori_loop(0, COLS * HEADS, query_one, 0)

    def query_finish(col, carry):
        raw = unit_back(window(qs, col, 2), q_inv[col] * SCALE, grads[col])
        for d in range(CH):
            raws[col, pl.ds(d * R, ROWS), :] = raw[d]
        return carry

    lax.fori_loop(0, COLS, query_finish, 0)

    def query_sums(half, carry):
        query_acc, out_acc = carry
        raw, mixed, normed_all, cot_all = [], [], [], []
        for row in (2 * half, 2 * half + 1):
            for j in range(2):
                raw.append(view(raws, j, row, CH))
                raw_query[row, j] = raw[-1]
                mixed.append(view(attended, j, row, CH))
                normed_all.append(normed[row, 2 + j])
                cot_all.append(cot[row, j])
        raw, mixed, normed_all, cot_all = (
            jnp.concatenate(x, axis=1) for x in (raw, mixed, normed_all, cot_all)
        )
        return query_acc + outer(normed_all, raw), out_acc + outer(mixed, cot_all)

    flat = jnp.zeros((CH, CH), F32)
    query_acc, out_acc = lax.fori_loop(0, ROWS // 2, query_sums, (flat, flat))
    weight_sums[CH : 2 * CH, :] = jnp.concatenate([query_acc, out_acc], axis=1)

    def key_step(acc, step, col, j, i, base, first_row):
        key_acc, value_acc = acc
        start = first_row - i + 2
        prob = probs[step, pl.ds((5 * j + i) * W + start, ROWS), :]
        score_grad = score_grads[step, pl.ds((5 * j + i) * W + start, ROWS), :]
        key_acc = [a + score_grad * take(qs, col, base + d * S + start) for d, a in enumerate(key_acc)]
        value_acc = [a + prob * take(ogs, col, base + d * S + start) for d, a in enumerate(value_acc)]
        return key_acc, value_acc

    edge_first, edge_offset = edge_row * 2 // 3, edge_row // 2

    def key_columns(view_col, head, cols):
        base = head * (SIZE * S)
        own_steps = [(i, 2) for i in range(5)]
        halo_steps = [(edge_offset + i, edge_first) for i in range(2)]
        for steps, key_ref, value_ref in (
            (own_steps, grads, raws), (halo_steps, halo_grads, halo_raws)
        ):
            acc = ([zeros] * SIZE, [zeros] * SIZE)
            for col in cols:
                for i, first_row in steps:
                    acc = key_step(acc, col * HEADS + head, col, view_col - col, i, base, first_row)
            for d in range(SIZE):
                key_ref[view_col, head * SIZE + d] = acc[0][d]
                value_ref[view_col, pl.ds((CH + head * SIZE + d) * R, ROWS), :] = acc[1][d]

    def inner_columns(step, carry):
        key_columns(1 + step // HEADS, step % HEADS, (0, 1))
        return carry

    def outer_columns(step, carry):
        side_col = step // HEADS
        key_columns(5 * side_col, step % HEADS, (side_col,))
        return carry

    lax.fori_loop(0, 4 * HEADS, inner_columns, 0)
    lax.fori_loop(0, 2 * HEADS, outer_columns, 0)

    def key_finish(col, carry):
        for source, target, row in ((grads, raws, 2), (halo_grads, halo_raws, edge_first)):
            scale = k_inv[col, pl.ds(row, ROWS), :] * SCALE
            raw = unit_back(window(ks, col, row), scale, source[col])
            for d in range(CH):
                target[col, pl.ds(d * R, ROWS), :] = raw[d]
        return carry

    lax.fori_loop(0, 6, key_finish, 0)

    w_keys = w_kv[...]

    def key_sums(source, from_row, targets):
        def one(row, acc):
            raw, normed_all = [], []
            for col in (first_col, second_col, 2):
                for j in range(2):
                    raw.append(view(source, col + j, row + from_row, 2 * CH))
                    normed_all.append(normed[row + (0 if source is raws else ROWS), col + j])
            shares = jnp.dot(
                w_keys, jnp.concatenate(raw[: 2 * len(targets)], axis=1), preferred_element_type=F32
            ).astype(BF16)
            for k, (target, first_row) in enumerate(targets):
                for j in range(2):
                    at = (2 * k + j) * PIX
                    target[row + first_row, j] = shares[:, at : at + PIX]
            if source is raws:
                for j in range(2):
                    own_raw[row, j] = raw[4 + j]
            return acc + outer(jnp.concatenate(normed_all, axis=1), jnp.concatenate(raw, axis=1))

        return one

    own_targets = ((to_first, 0), (to_second, 0))
    halo_targets = ((to_first, ROWS), (to_second, ROWS), (own_edge, 0))
    acc = lax.fori_loop(0, ROWS, key_sums(raws, 0, own_targets), jnp.zeros((CH, 2 * CH), F32))
    weight_sums[0:CH, :] = lax.fori_loop(0, 2, key_sums(halo_raws, edge_row, halo_targets), acc)


def row_kernel(own_edge, first_raw, second_raw, row_send, parts, sems):
    copies = [
        pltpu.make_async_copy(x.at[pl.ds(ROWS, 2)], parts.at[k], sems.at[k])
        for k, x in enumerate((first_raw, second_raw))
    ]
    for copy in copies:
        copy.start()
    for copy in copies:
        copy.wait()
    for row in range(2):
        for j in range(2):
            row_send[row, j] = (
                own_edge[row, j].astype(F32)
                + parts[0, row, j].astype(F32)
                + parts[1, row, j].astype(F32)
            ).astype(BF16)


def features_kernel(
    side, own_raw, first_raw, second_raw, row_raw, raw_query, feats, cot, gain, w_back,
    feats_grad, shared,
):
    _, _, edge_row = halo_start(side)

    def join(row):
        for j in range(2):
            shared[row, j] = first_raw[row, j].astype(F32) + second_raw[row, j].astype(F32)

    def join_edge(row):
        for j in range(2):
            shared[row + edge_row, j] = shared[row + edge_row, j] + row_raw[row, j].astype(F32)

    each_row(ROWS, (join,))
    each_row(2, (join_edge,))
    gain_full = gain[...]
    w_b = w_back[...]

    def view_row(row):
        raw = jnp.concatenate([pair(raw_query, row), pair(own_raw, row)], axis=0)
        own_grad = jnp.dot(w_b, raw, preferred_element_type=F32)
        for j in range(2):
            normed_grad = own_grad[:, j * PIX : (j + 1) * PIX] + shared[row, j]
            values = feats[row, j].astype(F32)
            inv_norm = inv_rms(values)
            scaled = values * inv_norm
            scaled_grad = normed_grad * gain_full
            mean = jnp.mean(scaled_grad * scaled, axis=0, keepdims=True)
            branch = inv_norm * (scaled_grad - scaled * mean)
            feats_grad[row, j] = (cot[row, j].astype(F32) + branch).astype(BF16)

    each_row(ROWS, (view_row,))


def last_kernel(factor, sums, w_q, w_kv, gain, query_grad, keyval_grad, output_grad, gain_grad):
    keyval = sums[0:CH, :] * factor
    rest = sums[CH : 2 * CH, :] * factor
    query = rest[:, :CH]
    keyval_grad[...] = keyval
    query_grad[...] = query
    output_grad[...] = rest[:, CH:]
    col = jnp.sum(query * w_q[...].astype(F32), axis=1, keepdims=True) + jnp.sum(
        keyval * w_kv[...].astype(F32), axis=1, keepdims=True
    )
    line = jnp.sum(jnp.where(eye(), jnp.broadcast_to(col, (CH, CH)), 0.0), axis=0, keepdims=True)
    gain_grad[...] = line / gain[...]


def call(kernel, outs, scratch, flops, *operands, aliases=(), far=()):
    return pl.pallas_call(
        kernel,
        out_shape=[jax.ShapeDtypeStruct(shape, dtype) for shape, dtype in outs],
        in_specs=[
            SM if x.dtype == jnp.int32 else FAR if k in far else VM for k, x in enumerate(operands)
        ],
        out_specs=[VM] * len(outs),
        scratch_shapes=[pltpu.VMEM(x, F32) if isinstance(x, tuple) else x for x in scratch],
        input_output_aliases=dict(aliases),
        compiler_params=pltpu.CompilerParams(vmem_limit_bytes=20 * 1024 * 1024),
        cost_estimate=pl.CostEstimate(flops=flops, bytes_accessed=1000000, transcendentals=0),
    )(*operands)


def near_memory(x):
    return pltpu.with_memory_space_constraint(x, pltpu.VMEM)


def sum_kernel(shares, copies):
    share = jnp.sum(shares[...].astype(F32), axis=0).astype(copies.dtype)
    for k in range(copies.shape[0]):
        copies[k] = share


def sum_everywhere(values):
    near, far = ("py", "pc", "vrow"), ("px", "vcol")
    near_count, far_count = (math.prod(lax.axis_size(a) for a in axes) for axes in (near, far))
    size = values.size // (near_count * PIX)

    def exchange(copies, axes):
        return near_memory(lax.all_to_all(copies, axes, 0, 0))

    shares = exchange(values.reshape(near_count, size, PIX), near)
    (copies,) = call(sum_kernel, [((far_count, size, PIX), BF16)], [], 100000, shares)
    shares = exchange(copies, far)
    (copies,) = call(sum_kernel, [((near_count, size, PIX), F32)], [], 100000, shares)
    return lax.all_to_all(copies, near, 0, 0).reshape(values.shape)


def layer(features, out_cotangent, norm_gain, query_proj, keyval_proj, output_proj):
    place = lax.axis_index("vrow") * 2 + jnp.bitwise_and(lax.axis_index("vcol"), 1)
    side = place.astype(jnp.int32).reshape(1)
    cols = lax.axis_size("vcol")
    grid = ("vrow", "vcol")

    def both_ways(pairs):
        return [*pairs, *((b, a) for a, b in pairs)]

    rounds = [[(i, i + 1) for i in range(start, cols - 1, 2)] for start in (0, 1)]
    first_swap, second_swap = (both_ways(pairs) for pairs in rounds)
    first_cross, second_cross = (
        [(a * cols + i, (1 - a) * cols + j) for a in (0, 1) for i, j in swap]
        for swap in (first_swap, second_swap)
    )
    row_swap = both_ways([(0, 1)])
    gain = norm_gain.reshape(1, CH)
    held = [
        pltpu.with_memory_space_constraint(x, pltpu.HBM)
        for x in (features, out_cotangent, gain, query_proj, keyval_proj, output_proj)
    ]

    views = ((ROWS, COLS, CH, PIX), BF16)
    edge, feats, cot, gain_row, w_q, w_kv, w_out = call(
        fetch_kernel,
        [
            ((2, COLS, CH, PIX), BF16), views, views, ((1, CH), F32), ((CH, CH), BF16),
            ((CH, 2 * CH), BF16), ((CH, CH), BF16),
        ],
        [pltpu.SemaphoreType.DMA((7,))], 1000, side, *held, far=(1, 2, 3, 4, 5, 6),
    )
    first_corner = lax.ppermute(edge, grid, first_cross)
    second_corner = lax.ppermute(edge, grid, second_cross)
    first = lax.ppermute(features, "vcol", first_swap)
    second = lax.ppermute(features, "vcol", second_swap)
    row_halo = lax.ppermute(edge, "vrow", row_swap)

    own = ((COLS, CH * S, PIX), F32)
    padded = ((6, CH * S, PIX), F32)
    lanes = ((COLS, ROWS, PIX), F32)
    key_lanes = ((6, 16, PIX), F32)
    steps = COLS * HEADS
    offsets = ((steps, 25, ROWS, PIX), F32)
    all_views = ((ROWS + 2, 6, CH, PIX), BF16)
    shares = ((ROWS + 2, COLS, CH, PIX), BF16)
    qs, ks, vs, ogs, q_inv, k_inv, normed, gain_full, w_in, w_back = call(
        own_kernel,
        [
            own, padded, padded, own, lanes, key_lanes, all_views, ((CH, PIX), F32),
            ((3 * CH, CH), BF16), ((CH, 3 * CH), BF16),
        ],
        [], 2000000,
        side, feats, cot, gain_row, w_q, w_kv, w_out,
    )
    ks, vs, k_inv, normed, weights, prob_grads, attended, stats = call(
        forward_kernel,
        [
            padded, padded, key_lanes, all_views, offsets, offsets,
            ((COLS, CH * R, PIX), F32), ((2, steps, ROWS, PIX), F32),
        ],
        [], 4000000,
        side, first, second, row_halo, first_corner, second_corner, gain_full, w_in, ogs, qs,
        ks, vs, k_inv, normed,
        aliases=((10, 0), (11, 1), (12, 2), (13, 3)),
    )
    weight_sums, raw_query, to_first, to_second, own_raw, own_edge = call(
        gradient_kernel,
        [
            ((2 * CH, PIX), F32), views, shares, shares, ((ROWS, COLS, 2 * CH, PIX), BF16),
            ((2, COLS, CH, PIX), BF16),
        ],
        [
            (steps, 25 * W, PIX), (steps, 25 * W, PIX), (6, CH, ROWS, PIX), (6, 2 * CH * R, PIX),
            (6, CH, ROWS, PIX), (6, 2 * CH * R, PIX),
        ],
        5000000,
        side, qs, ks, ogs, q_inv, k_inv, normed, weights, prob_grads, attended, stats, cot, w_kv,
    )
    sums = sum_everywhere(weight_sums)
    first_raw, second_raw = (
        lax.ppermute(pltpu.with_memory_space_constraint(x, pltpu.HBM), "vcol", swap)
        for x, swap in ((to_first, first_swap), (to_second, second_swap))
    )
    (row_send,) = call(
        row_kernel, [((2, COLS, CH, PIX), BF16)],
        [pltpu.VMEM((2, 2, COLS, CH, PIX), BF16), pltpu.SemaphoreType.DMA((2,))], 10000,
        own_edge, first_raw, second_raw, far=(1, 2),
    )
    row_raw = lax.ppermute(row_send, "vrow", row_swap)
    (features_grad,) = call(
        features_kernel, [views], [(ROWS, COLS, CH, PIX)], 2000000,
        side, own_raw, first_raw, second_raw, row_raw, raw_query, feats, cot, gain_full, w_back,
    )
    tokens_all = ROWS * COLS * PIX * math.prod(lax.axis_size(a) for a in AXES)
    query_grad, keyval_grad, output_grad, gain_grad = call(
        functools.partial(last_kernel, 1.0 / math.sqrt(tokens_all)),
        [((CH, CH), F32), ((CH, 2 * CH), F32), ((CH, CH), F32), ((1, CH), F32)],
        [], 100000,
        sums, w_q, w_kv, gain_row,
    )
    return features_grad, query_grad, keyval_grad, output_grad, gain_grad.reshape(CH)


def solution(mesh):
    rows, cols, _ = mesh.devices.shape
    parts = jax.sharding.Mesh(mesh.devices.reshape(rows, cols, 4, 4, 2), AXES)
    placed = P("vrow", "vcol", None, AXES[2:])
    return jax.shard_map(
        layer,
        mesh=parts,
        in_specs=(placed, placed, P(), P(), P(), P()),
        out_specs=(placed, P(), P(), P(), P()),
        check_vma=False,
    )
```
